256 devices in a mesh: pair: 8 (over y_lo, x), feat: 32 (over y_hi, z, core).
Axes of the slice: x: 4, y: 4 (y_hi: 2, y_lo: 2; y = y_hi * 2 + y_lo), z: 8, core: 2. Of those that a mesh axis runs over, the one named last changes fastest.
Arguments:
- decoder: float32 [8, 16384, 2048], P('pair', 'feat'), may hold values from -0.3125 to 0.3125
- pair_map: int32 [8, 2], P('pair'), may hold values from 0 to 3, as said below
- indices: int32 [3, 256, 128], replicated, may hold values from 0 to 16383, as said below
- values: float32 [3, 256, 128], replicated, may hold values from 0.2 to 3
- target: float32 [3, 256, 2048], P(None, ('pair', 'feat')), may hold values from -6 to 6
Outputs:
- recon: bfloat16 [3, 256, 2048], P(None, ('pair', 'feat'))
- dec_grad: float32 [8, 16384, 2048], P('pair', 'feat')
- feat_grad: float32 [3, 256, 128], P(None, ('pair', 'feat'))
The draws below stay inside these ranges and needn't reach their ends.
Inputs may be any that keep to these rules, and one draw needn't show every extreme that they name: `pair_map`: each pair (s, t) of layers with s <= t < 3 stands in exactly one row as (s, t); every other row is (3, 3), an empty slot. For each layer and token the 128 indices are distinct.
All inputs are finite; a program needn't handle non-finite values.
Results may differ from the reference program's by a relative error of at most 0.0027.
Values may be sent and summed in bfloat16 or wider, within the bound.
A program may use at most 128 MiB of HBM per device.

```python
import math
import jax
import jax.numpy as jnp
import numpy as np
from jax import lax

D = 2048
F = 16384
L = 3
K = 128
TOK = 256
SLOTS = 8


def draw_indices(key, part):
    scores = jax.random.randint(key, (L, TOK, F), 0, 2 ** 30)
    ranked = jnp.argsort(scores, axis=-1, stable=True)
    return ranked[:, :, :K].astype(jnp.int32)


def draw_pair_map(key, part):
    listing = [(source, target_layer) for target_layer in range(L) for source in range(target_layer + 1)]
    listing = listing + [(L, L)] * (SLOTS - len(listing))
    table = jnp.asarray(np.array(listing, dtype=np.int32))
    shuffled = jax.random.permutation(jax.random.fold_in(key, 7), SLOTS)
    return table[shuffled].astype(jnp.int32)


def level_of(rng, dims, cuts, least, largest):
    loudness = 1.0
    for axis_at, blocks in cuts:
        heights = jax.random.uniform(jax.random.fold_in(jax.random.fold_in(rng, 6), axis_at), (blocks,), jnp.float32, least / len(cuts), largest / len(cuts))
        loudness = loudness * jnp.repeat(jnp.exp(heights), dims[axis_at] // blocks).reshape((-1,) + (1,) * (len(dims) - 1 - axis_at))
    return loudness


def gaussian(rng, extent, width, limit, split=(), kind=jnp.bfloat16):
    level = level_of(rng, extent, split, -0.22, 0.18) if split else 1.0
    values = jax.random.normal(rng, extent, jnp.float32) * width * level
    return jnp.minimum(jnp.maximum(values, -limit), limit).astype(kind)


def setup_inputs(seed: int = 0) -> dict:
    key_of = jax.random.split(jax.random.key(seed), 6)
    decoder = gaussian(key_of[0], (SLOTS, F, D), (K * L) ** -0.5, 0.3125, ((0, 8), (1, 32)), jnp.float32)
    pair_map = draw_pair_map(jax.random.fold_in(key_of[5], 71), 0)
    indices = draw_indices(jax.random.fold_in(key_of[5], 71), 0)
    values = jnp.clip(jnp.exp(jax.random.uniform(key_of[3], (L, TOK, K), jnp.float32, math.log(0.2), math.log(3.0))), 0.2, 3.0)
    target = gaussian(key_of[4], (L, TOK, D), 1.0, 6.0, ((1, 256),), jnp.float32)
    return dict(decoder=decoder, pair_map=pair_map, indices=indices, values=values, target=target)


def reference(decoder, pair_map, indices, values, target):
    layer_axis = jnp.arange(L, dtype=jnp.int32)[:, None, None]
    token_axis = jnp.arange(TOK, dtype=jnp.int32)[None, :, None]
    dense_acts = jnp.zeros((L, TOK, F), jnp.float32).at[layer_axis, token_axis, indices].set(values)
    sources = pair_map[:, 0]
    targets = pair_map[:, 1]

    def recon_step(running, slot_data):
        decoder_tile, source, target_layer = slot_data
        picked = jnp.minimum(source, L - 1)
        product = jnp.dot(dense_acts[picked], decoder_tile, precision=lax.Precision.HIGHEST, preferred_element_type=jnp.float32)
        choose = jax.nn.one_hot(target_layer, L, dtype=jnp.float32)
        return running + choose[:, None, None] * product[None], None

    full, _ = lax.scan(recon_step, jnp.zeros((L, TOK, D), jnp.float32), (decoder, sources, targets))
    recon = full.astype(jnp.bfloat16)
    error = (full - target).astype(jnp.bfloat16)
    error_wide = error.astype(jnp.float32)

    def grad_step(grad_dense, slot_data):
        decoder_tile, source, target_layer = slot_data
        is_live = (target_layer < L).astype(jnp.float32)
        picked = jnp.minimum(source, L - 1)
        slot_error = error_wide[jnp.minimum(target_layer, L - 1)] * is_live
        tile_grad = jnp.dot(dense_acts[picked].T, slot_error, precision=lax.Precision.HIGHEST, preferred_element_type=jnp.float32)
        back = jnp.dot(slot_error, decoder_tile.T, precision=lax.Precision.HIGHEST, preferred_element_type=jnp.float32)
        choose = jax.nn.one_hot(source, L, dtype=jnp.float32)
        return grad_dense + choose[:, None, None] * back[None], tile_grad

    grad_dense, dec_grad = lax.scan(grad_step, jnp.zeros((L, TOK, F), jnp.float32), (decoder, sources, targets))
    feat_grad = jnp.take_along_axis(grad_dense, indices, axis=2)
    return recon, dec_grad, feat_grad
```

```python
import jax
import jax.numpy as jnp
from jax import lax
from jax.experimental import pallas as pl
from jax.experimental.pallas import tpu as pltpu
from jax.sharding import PartitionSpec as P

MESH = pl.DeviceIdType.MESH
F32 = jnp.float32
BF16 = jnp.bfloat16

LAYERS = 3
TOK = 256
ACTIVE = 128
WIDTH = 512
MODEL = 2048
HALF = MODEL // 2
PAIRS = 8
PLANE = 16
LINE = 16
ROWS = TOK // PLANE


def split(x):
    high = x.astype(BF16)
    return high, (x - high.astype(F32)).astype(BF16)


def nt(a, b):
    return lax.dot_general(a, b, (((1,), (1,)), ((), ())), preferred_element_type=F32)


def exchange_kernel(
    pair_map, indices, values, target, decoder,
    recon, feat, error_out, acts_high_t, acts_low_t,
    dec, dec_high, dec_low, ids_t, vals_t, acts_t, acts_high, acts_low,
    map_send, map_rx, part_send, part_rx, part_own, plane_rx, layer_sum,
    line_send, line_rx, err_send, err_rx, err_wide, err_layers, err_pick, err,
    back, picked, pick_rx, pick_line, feat_rx,
    dec_sem, map_ssem, map_rsem, part_ssem, part_rsem, plane_ssem, plane_rsem,
    line_ssem, line_rsem, err_ssem, err_rsem, spread_ssem, spread_rsem,
    relay_ssem, relay_rsem, pick_ssem, pick_rsem, feat_ssem, feat_rsem,
):
    p = lax.axis_index("pair")
    f = lax.axis_index("feat")
    y = f // 16
    w = lax.rem(f, 16)
    core = lax.rem(f, 2)
    q = p * 2 + y

    def plane_peer(d):
        q2 = lax.rem(q + d, PLANE)
        return q2, (q2 // 2, lax.rem(q2, 2) * 16 + w)

    def line_peer(d):
        w2 = lax.rem(w + d, LINE)
        return w2, (p, y * 16 + w2)

    partner = (p, f + 1 - 2 * core)

    for block in range(4):
        cols = pl.ds(block * 512, 512)
        pltpu.make_async_copy(
            decoder.at[0, :, cols], dec.at[:, cols], dec_sem.at[block]
        ).start()

    barrier = pltpu.get_barrier_semaphore()

    @pl.loop(1, 16)
    def _(d):
        pl.semaphore_signal(barrier, inc=1, device_id=plane_peer(d)[1], device_id_type=MESH)
        pl.semaphore_signal(barrier, inc=1, device_id=line_peer(d)[1], device_id_type=MESH)

    pl.semaphore_wait(barrier, 30)

    source = pair_map[0, 0]
    goal = pair_map[0, 1]
    row = lax.broadcasted_iota(jnp.int32, (8, 128), 0)
    tile = jnp.where(row < 4, source, goal)
    map_send[...] = tile
    map_rx[p] = tile

    def map_copy(d):
        p2 = lax.rem(p + d, PAIRS)
        return pltpu.make_async_remote_copy(
            src_ref=map_send, dst_ref=map_rx.at[p], send_sem=map_ssem.at[p2],
            recv_sem=map_rsem.at[p], device_id=(p2, f), device_id_type=MESH)

    def map_arrival(d):
        p2 = lax.rem(p + d, PAIRS)
        return pltpu.make_async_remote_copy(
            src_ref=map_send, dst_ref=map_rx.at[p2], send_sem=map_ssem.at[p],
            recv_sem=map_rsem.at[p2], device_id=(p2, f), device_id_type=MESH)

    @pl.loop(1, PAIRS)
    def _(d):
        map_copy(d).start()

    layer = jnp.minimum(source, LAYERS - 1)
    local = indices[layer] - f * WIDTH
    ids_t[...] = local.T
    vals_t[...] = values[layer].T

    @pl.loop(0, WIDTH // 64)
    def _(block):
        base = block * 64
        features = lax.broadcasted_iota(jnp.int32, (64, TOK), 0) + base

        def step(k, total):
            for j in range(4):
                ids = ids_t[pl.ds(k * 4 + j, 1), :]
                vals = vals_t[pl.ds(k * 4 + j, 1), :]
                total = jnp.where(ids == features, vals, total)
            return total

        total = lax.fori_loop(0, ACTIVE // 4, step, jnp.zeros((64, TOK), F32))
        acts_t[pl.ds(base, 64), :] = total
        high, low = split(total)
        acts_high_t[pl.ds(base, 64), :] = high
        acts_low_t[pl.ds(base, 64), :] = low

    for block in range(WIDTH // 128):
        cols = slice(block * 128, block * 128 + 128)
        high, low = split(acts_t[cols, :].T)
        acts_high[:, cols] = high
        acts_low[:, cols] = low

    for block in range(4):
        cols = pl.ds(block * 512, 512)
        pltpu.make_async_copy(
            decoder.at[0, :, cols], dec.at[:, cols], dec_sem.at[block]
        ).wait()

    @pl.loop(0, WIDTH // 16)
    def _(block):
        rows = pl.ds(block * 16, 16)
        high, low = split(dec[rows, :])
        dec_high[rows, :] = high
        dec_low[rows, :] = low

    def partial(cols):
        high = dec_high[:, cols]
        return (
            jnp.dot(acts_high[...], high, preferred_element_type=F32)
            + jnp.dot(acts_low[...], high, preferred_element_type=F32)
            + jnp.dot(acts_high[...], dec_low[:, cols], preferred_element_type=F32)
        )

    part_copy = pltpu.make_async_remote_copy(
        src_ref=part_send, dst_ref=part_rx, send_sem=part_ssem, recv_sem=part_rsem,
        device_id=partner, device_id_type=MESH)

    @pl.loop(0, HALF // 256)
    def _(n):
        cols = pl.ds(pl.multiple_of((1 - core) * HALF + n * 256, 256), 256)
        part_send[:, pl.ds(pl.multiple_of(n * 256, 256), 256)] = partial(cols)

    part_copy.start()

    @pl.loop(0, HALF // 256)
    def _(n):
        cols = pl.ds(pl.multiple_of(core * HALF + n * 256, 256), 256)
        part_own[:, pl.ds(pl.multiple_of(n * 256, 256), 256)] = partial(cols)

    part_copy.wait()

    def rows_of(q2):
        return pl.ds(pl.multiple_of(q2 * ROWS, ROWS), ROWS)

    def plane_copy(d):
        q2, peer = plane_peer(d)
        return pltpu.make_async_remote_copy(
            src_ref=part_own.at[rows_of(q2)], dst_ref=plane_rx.at[q], send_sem=plane_ssem.at[q2],
            recv_sem=plane_rsem.at[q], device_id=peer, device_id_type=MESH)

    def plane_arrival(q2):
        return pltpu.make_async_remote_copy(
            src_ref=part_own.at[rows_of(q2)], dst_ref=plane_rx.at[q2], send_sem=plane_ssem.at[q],
            recv_sem=plane_rsem.at[q2], device_id=partner, device_id_type=MESH)

    @pl.loop(1, PLANE)
    def _(d):
        rows = rows_of(lax.rem(q + d, PLANE))
        part_own[rows, :] = part_own[rows, :] + part_rx[rows, :]
        plane_copy(d).start()

    plane_rx[q] = part_own[rows_of(q), :] + part_rx[rows_of(q), :]

    @pl.loop(1, PAIRS)
    def _(d):
        map_arrival(d).wait_recv()

    @pl.loop(1, PLANE)
    def _(d):
        plane_arrival(lax.rem(q + d, PLANE)).wait_recv()

    layer_sum[...] = jnp.zeros_like(layer_sum)

    @pl.loop(0, PAIRS)
    def _(p2):
        both = plane_rx[2 * p2] + plane_rx[2 * p2 + 1]
        goal2 = map_rx[p2, 4:5, 0:1]
        for l in range(LAYERS):
            layer_sum[l] += jnp.where(goal2 == l, both, 0.0)

    for l in range(LAYERS):
        for m in range(8):
            line_send[pl.ds(l * 8 + m, 16, stride=24), :] = layer_sum[l, :, m * 128:m * 128 + 128]

    def tile_of(w2):
        return pl.ds(pl.multiple_of(w2 * 24, 8), 24)

    def line_copy(d):
        w2, peer = line_peer(d)
        return pltpu.make_async_remote_copy(
            src_ref=line_send.at[tile_of(w2)], dst_ref=line_rx.at[w], send_sem=line_ssem.at[w2],
            recv_sem=line_rsem.at[w], device_id=peer, device_id_type=MESH)

    def line_arrival(w2):
        return pltpu.make_async_remote_copy(
            src_ref=line_send.at[tile_of(w2)], dst_ref=line_rx.at[w2], send_sem=line_ssem.at[w],
            recv_sem=line_rsem.at[w2], device_id=partner, device_id_type=MESH)

    @pl.loop(1, LINE)
    def _(d):
        line_copy(d).start()

    line_rx[w] = line_send[tile_of(w), :]

    @pl.loop(1, LINE)
    def _(d):
        line_arrival(lax.rem(w + d, LINE)).wait_recv()

    for half in range(2):
        total = line_rx[half]
        for z2 in range(1, 8):
            total = total + line_rx[2 * z2 + half]
        for l in range(LAYERS):
            part = total[l * 8:l * 8 + 8]
            rows = slice(half * 8, half * 8 + 8)
            recon[l, rows, :] = part.astype(BF16)
            err_send[half, l * 8:l * 8 + 8, :] = (part - target[l, rows, :]).astype(BF16)
        err_send[half, 24:32, :] = jnp.zeros((8, 128), BF16)

    def err_copy(d):
        w2, peer = line_peer(d)
        return pltpu.make_async_remote_copy(
            src_ref=err_send.at[lax.rem(w2, 2)], dst_ref=err_rx.at[w], send_sem=err_ssem.at[w2],
            recv_sem=err_rsem.at[w], device_id=peer, device_id_type=MESH)

    def err_arrival(w2):
        return pltpu.make_async_remote_copy(
            src_ref=err_send.at[0], dst_ref=err_rx.at[w2], send_sem=err_ssem.at[w],
            recv_sem=err_rsem.at[w2], device_id=partner, device_id_type=MESH)

    @pl.loop(1, LINE)
    def _(d):
        err_copy(d).start()

    err_rx[w] = err_send[core]

    @pl.loop(1, LINE)
    def _(d):
        err_arrival(lax.rem(w + d, LINE)).wait_recv()

    @pl.loop(0, LINE)
    def _(w2):
        err_wide[pl.ds(pl.multiple_of(w2 * 32, 32), 32), :] = err_rx[w2].astype(F32)

    for l in range(LAYERS):
        for m in range(8):
            err_layers[l, :, m * 128:m * 128 + 128] = err_wide[pl.ds(l * 8 + m, 16, stride=32), :]

    @pl.loop(0, PAIRS)
    def _(p2):
        goal2 = map_rx[p2, 4:5, 0:1]
        chosen = jnp.zeros((ROWS, HALF), F32)
        for l in range(LAYERS):
            chosen = jnp.where(goal2 == l, err_layers[l], chosen)
        err_pick[p2] = chosen.astype(BF16)

    def spread_copy(d):
        q2, peer = plane_peer(d)
        return pltpu.make_async_remote_copy(
            src_ref=err_pick.at[q2 // 2], dst_ref=err.at[core, rows_of(q)], send_sem=spread_ssem.at[q2],
            recv_sem=spread_rsem.at[q], device_id=peer, device_id_type=MESH)

    def spread_arrival(q2):
        return pltpu.make_async_remote_copy(
            src_ref=err_pick.at[0], dst_ref=err.at[core, rows_of(q2)], send_sem=spread_ssem.at[q],
            recv_sem=spread_rsem.at[q2], device_id=partner, device_id_type=MESH)

    def relay_copy(q2):
        piece = err.at[core, rows_of(q2)]
        return pltpu.make_async_remote_copy(
            src_ref=piece, dst_ref=piece, send_sem=relay_ssem.at[q2],
            recv_sem=relay_rsem.at[q2], device_id=partner, device_id_type=MESH)

    def relay_arrival(q2):
        piece = err.at[1 - core, rows_of(q2)]
        return pltpu.make_async_remote_copy(
            src_ref=piece, dst_ref=piece, send_sem=relay_ssem.at[q2],
            recv_sem=relay_rsem.at[q2], device_id=partner, device_id_type=MESH)

    @pl.loop(1, PLANE)
    def _(d):
        spread_copy(d).start()

    err[core, rows_of(q), :] = err_pick[p]
    relay_copy(q).start()

    @pl.loop(1, PLANE)
    def _(d):
        q2 = lax.rem(q + d, PLANE)
        spread_arrival(q2).wait_recv()
        relay_copy(q2).start()

    @pl.loop(0, PLANE)
    def _(q2):
        relay_arrival(q2).wait_recv()

    error_out[...] = err[...]

    @pl.loop(0, WIDTH // 128)
    def _(n):
        rows = pl.ds(pl.multiple_of(n * 128, 128), 128)
        total = jnp.zeros((TOK, 128), F32)
        for half in range(2):
            cols = slice(half * HALF, half * HALF + HALF)
            total = total + nt(err[half], dec_high[rows, cols]) + nt(err[half], dec_low[rows, cols])
        back[n] = total

    local = indices[layer] - f * WIDTH
    lane = jnp.bitwise_and(local, 127)
    block_of = jnp.right_shift(local, 7)
    found = jnp.zeros((TOK, ACTIVE), F32)
    for n in range(WIDTH // 128):
        here = jnp.take_along_axis(back[n], lane, axis=1)
        found = jnp.where(block_of == n, here, found)
    picked[...] = found

    def pick_copy(d):
        q2, peer = plane_peer(d)
        return pltpu.make_async_remote_copy(
            src_ref=picked.at[rows_of(q2)], dst_ref=pick_rx.at[q], send_sem=pick_ssem.at[q2],
            recv_sem=pick_rsem.at[q], device_id=peer, device_id_type=MESH)

    def pick_arrival(q2):
        return pltpu.make_async_remote_copy(
            src_ref=picked.at[rows_of(q2)], dst_ref=pick_rx.at[q2], send_sem=pick_ssem.at[q],
            recv_sem=pick_rsem.at[q2], device_id=partner, device_id_type=MESH)

    @pl.loop(1, PLANE)
    def _(d):
        pick_copy(d).start()

    pick_rx[q] = picked[rows_of(q), :]
    pick_line[...] = jnp.zeros_like(pick_line)

    @pl.loop(1, PLANE)
    def _(d):
        pick_arrival(lax.rem(q + d, PLANE)).wait_recv()

    sums = [jnp.zeros((ROWS, ACTIVE), F32) for _ in range(LAYERS)]
    for p2 in range(PAIRS):
        both = pick_rx[2 * p2] + pick_rx[2 * p2 + 1]
        source2 = map_rx[p2, 0:1, 0:1]
        for l in range(LAYERS):
            sums[l] = sums[l] + jnp.where(source2 == l, both, 0.0)
    for l in range(LAYERS):
        pick_line[pl.ds(l, 16, stride=8), :] = sums[l]

    def feat_copy(d):
        w2, peer = line_peer(d)
        return pltpu.make_async_remote_copy(
            src_ref=pick_line.at[pl.ds(pl.multiple_of(w2 * 8, 8), 8)], dst_ref=feat_rx.at[w],
            send_sem=feat_ssem.at[w2], recv_sem=feat_rsem.at[w], device_id=peer, device_id_type=MESH)

    def feat_arrival(w2):
        return pltpu.make_async_remote_copy(
            src_ref=pick_line.at[pl.ds(0, 8)], dst_ref=feat_rx.at[w2],
            send_sem=feat_ssem.at[w], recv_sem=feat_rsem.at[w2], device_id=partner, device_id_type=MESH)

    @pl.loop(1, LINE)
    def _(d):
        feat_copy(d).start()

    feat_rx[w] = pick_line[pl.ds(pl.multiple_of(w * 8, 8), 8), :]

    @pl.loop(1, LINE)
    def _(d):
        feat_arrival(lax.rem(w + d, LINE)).wait_recv()

    total = feat_rx[0]
    for w2 in range(1, LINE):
        total = total + feat_rx[w2]
    feat[...] = total[0:LAYERS]

    @pl.loop(1, PAIRS)
    def _(d):
        map_copy(d).wait_send()

    @pl.loop(1, 16)
    def _(d):
        plane_copy(d).wait_send()
        line_copy(d).wait_send()
        err_copy(d).wait_send()
        spread_copy(d).wait_send()
        pick_copy(d).wait_send()
        feat_copy(d).wait_send()

    @pl.loop(0, PLANE)
    def _(q2):
        relay_copy(q2).wait_send()


def grad_kernel(acts_high_t, acts_low_t, err, out):
    e = err[0]
    out[...] = (
        jnp.dot(acts_high_t[...], e, preferred_element_type=F32)
        + jnp.dot(acts_low_t[...], e, preferred_element_type=F32)
    )


def body(decoder, pair_map, indices, values, target):
    vmem = pl.BlockSpec(memory_space=pltpu.VMEM)
    dma = pltpu.SemaphoreType.DMA
    recon, feat, err, acts_high_t, acts_low_t = pl.pallas_call(
        exchange_kernel,
        out_shape=(
            jax.ShapeDtypeStruct((LAYERS, 16, 128), BF16),
            jax.ShapeDtypeStruct((LAYERS, ACTIVE), F32),
            jax.ShapeDtypeStruct((2, TOK, HALF), BF16),
            jax.ShapeDtypeStruct((WIDTH, TOK), BF16),
            jax.ShapeDtypeStruct((WIDTH, TOK), BF16),
        ),
        in_specs=[pl.BlockSpec(memory_space=pltpu.SMEM), vmem, vmem, vmem, pl.BlockSpec(memory_space=pl.ANY)],
        out_specs=(vmem,) * 5,
        scratch_shapes=[
            pltpu.VMEM((WIDTH, MODEL), F32),
            pltpu.VMEM((WIDTH, MODEL), BF16),
            pltpu.VMEM((WIDTH, MODEL), BF16),
            pltpu.VMEM((ACTIVE, TOK), jnp.int32),
            pltpu.VMEM((ACTIVE, TOK), F32),
            pltpu.VMEM((WIDTH, TOK), F32),
            pltpu.VMEM((TOK, WIDTH), BF16),
            pltpu.VMEM((TOK, WIDTH), BF16),
            pltpu.VMEM((8, 128), jnp.int32),
            pltpu.VMEM((PAIRS, 8, 128), jnp.int32),
            pltpu.VMEM((TOK, HALF), F32),
            pltpu.VMEM((TOK, HALF), F32),
            pltpu.VMEM((TOK, HALF), F32),
            pltpu.VMEM((PLANE, ROWS, HALF), F32),
            pltpu.VMEM((LAYERS, ROWS, HALF), F32),
            pltpu.VMEM((LINE * 24, 128), F32),
            pltpu.VMEM((LINE, 24, 128), F32),
            pltpu.VMEM((2, 32, 128), BF16),
            pltpu.VMEM((LINE, 32, 128), BF16),
            pltpu.VMEM((LINE * 32, 128), F32),
            pltpu.VMEM((LAYERS, ROWS, HALF), F32),
            pltpu.VMEM((PAIRS, ROWS, HALF), BF16),
            pltpu.VMEM((2, TOK, HALF), BF16),
            pltpu.VMEM((WIDTH // 128, TOK, 128), F32),
            pltpu.VMEM((TOK, ACTIVE), F32),
            pltpu.VMEM((PLANE, ROWS, ACTIVE), F32),
            pltpu.VMEM((LINE * 8, 128), F32),
            pltpu.VMEM((LINE, 8, 128), F32),
            dma((4,)),
            dma((PAIRS,)), dma((PAIRS,)),
            dma, dma,
            dma((PLANE,)), dma((PLANE,)),
            dma((LINE,)), dma((LINE,)),
            dma((LINE,)), dma((LINE,)),
            dma((PLANE,)), dma((PLANE,)),
            dma((PLANE,)), dma((PLANE,)),
            dma((PLANE,)), dma((PLANE,)),
            dma((LINE,)), dma((LINE,)),
        ],
        compiler_params=pltpu.CompilerParams(
            collective_id=0, has_side_effects=True, vmem_limit_bytes=56 * 2**20
        ),
    )(pair_map, indices, values, target.reshape(LAYERS, 16, 128), decoder)
    dec_grad = pl.pallas_call(
        grad_kernel,
        grid=(8,),
        out_shape=jax.ShapeDtypeStruct((WIDTH, MODEL), F32),
        in_specs=[
            pl.BlockSpec((WIDTH, TOK), lambda n: (0, 0)),
            pl.BlockSpec((WIDTH, TOK), lambda n: (0, 0)),
            pl.BlockSpec((1, TOK, 256), lambda n: (n // 4, 0, n % 4)),
        ],
        out_specs=pl.BlockSpec((WIDTH, 256), lambda n: (0, n)),
    )(acts_high_t, acts_low_t, err)
    return (
        recon.reshape(LAYERS, 1, MODEL),
        dec_grad.reshape(1, WIDTH, MODEL),
        feat.reshape(LAYERS, 1, ACTIVE),
    )


def solution(mesh):
    in_specs = (P("pair", "feat", None), P("pair", None), P(), P(), P(None, ("pair", "feat"), None))
    out_specs = (
        P(None, ("pair", "feat"), None),
        P("pair", "feat", None),
        P(None, ("pair", "feat"), None),
    )
    return jax.shard_map(body, mesh=mesh, in_specs=in_specs, out_specs=out_specs, check_vma=False)
```

```python
import jax
import jax.numpy as jnp
from jax import lax
from jax.experimental import pallas as pl
from jax.experimental.pallas import tpu as pltpu
from jax.sharding import PartitionSpec as P

MESH = pl.DeviceIdType.MESH
F32 = jnp.float32
BF16 = jnp.bfloat16

LAYERS = 3
TOK = 256
ACTIVE = 128
WIDTH = 512
MODEL = 2048
HALF = MODEL // 2
PAIRS = 8
PLANE = 16
LINE = 16
ROWS = TOK // PLANE


def split(x):
    high = x.astype(BF16)
    return high, (x - high.astype(F32)).astype(BF16)


def nt(a, b):
    return lax.dot_general(a, b, (((1,), (1,)), ((), ())), preferred_element_type=F32)


def exchange_kernel(
    pair_map, indices, values, target, decoder,
    recon, feat, error_out, acts_high_out, acts_low_out,
    acts_high_t, acts_low_t, dec, dec_high, dec_low, ids_t, vals_t, acts_t, acts_high, acts_low,
    map_send, map_rx, part_send, part_rx, part_own, scale_send, scale_rx, plane_send, plane_rx, layer_sum,
    line_wide,
    line_send, line_rx, err_send, err_rx, err_wide, err_layers, err_pick, err,
    back, picked, pick_rx, pick_line, feat_rx,
    dec_sem, out_sem, map_ssem, map_rsem, part_ssem, part_rsem, scale_ssem, scale_rsem, plane_ssem, plane_rsem,
    line_ssem, line_rsem, err_ssem, err_rsem, spread_ssem, spread_rsem,
    relay_ssem, relay_rsem, pick_ssem, pick_rsem, feat_ssem, feat_rsem,
):
    p = lax.axis_index("pair")
    f = lax.axis_index("feat")
    y = f // 16
    w = lax.rem(f, 16)
    core = lax.rem(f, 2)
    q = p * 2 + y

    def plane_peer(i):
        a, b = i // 4, lax.rem(i, 4)
        far = 2 + jnp.where(a == 1, 3, jnp.where(a == 2, 1, jnp.where(a == 3, 2, 0)))
        x2 = lax.rem(lax.rem(p, 4) + far, 4)
        low2 = lax.rem(p // 4 + jnp.where((b == 1) | (b == 2), 1, 0), 2)
        y2 = lax.rem(y + jnp.where((b == 0) | (b == 2), 1, 0), 2)
        p2 = low2 * 4 + x2
        return p2 * 2 + y2, (p2, y2 * 16 + w)

    def line_peer(i):
        a, b = i // 2, lax.rem(i, 2)
        far = 4 + jnp.where(lax.rem(a, 2) == 1, 8 - (a + 1) // 2, a // 2)
        w2 = lax.rem(w // 2 + far, 8) * 2 + lax.rem(core + 1 - b, 2)
        return w2, (p, y * 16 + w2)

    partner = (p, f + 1 - 2 * core)

    for block in range(4):
        cols = pl.ds(block * 512, 512)
        pltpu.make_async_copy(
            decoder.at[0, :, cols], dec.at[:, cols], dec_sem.at[block]
        ).start()

    barrier = pltpu.get_barrier_semaphore()

    @pl.loop(0, 15)
    def _(d):
        pl.semaphore_signal(barrier, inc=1, device_id=plane_peer(d)[1], device_id_type=MESH)
        pl.semaphore_signal(barrier, inc=1, device_id=line_peer(d)[1], device_id_type=MESH)

    source = pair_map[0, 0]
    goal = pair_map[0, 1]
    row = lax.broadcasted_iota(jnp.int32, (8, 128), 0)
    tile = jnp.where(row < 4, source, goal)
    map_send[...] = tile
    map_rx[p] = tile

    def map_copy(d):
        p2 = lax.rem(p + d, PAIRS)
        return pltpu.make_async_remote_copy(
            src_ref=map_send, dst_ref=map_rx.at[p], send_sem=map_ssem.at[p2],
            recv_sem=map_rsem.at[p], device_id=(p2, f), device_id_type=MESH)

    def map_arrival(d):
        p2 = lax.rem(p + d, PAIRS)
        return pltpu.make_async_remote_copy(
            src_ref=map_send, dst_ref=map_rx.at[p2], send_sem=map_ssem.at[p],
            recv_sem=map_rsem.at[p2], device_id=(p2, f), device_id_type=MESH)

    layer = jnp.minimum(source, LAYERS - 1)
    local = indices[layer] - f * WIDTH
    ids_t[...] = local.T
    vals_t[...] = values[layer].T

    @pl.loop(0, WIDTH // 64)
    def _(block):
        base = block * 64
        features = lax.broadcasted_iota(jnp.int32, (64, TOK), 0) + base

        def step(k, total):
            for j in range(4):
                ids = ids_t[pl.ds(k * 4 + j, 1), :]
                vals = vals_t[pl.ds(k * 4 + j, 1), :]
                total = jnp.where(ids == features, vals, total)
            return total

        total = lax.fori_loop(0, ACTIVE // 4, step, jnp.zeros((64, TOK), F32))
        acts_t[pl.ds(base, 64), :] = total
        high, low = split(total)
        acts_high_t[pl.ds(base, 64), :] = high
        acts_low_t[pl.ds(base, 64), :] = low

    acts_copies = (
        pltpu.make_async_copy(acts_high_t, acts_high_out, out_sem.at[0]),
        pltpu.make_async_copy(acts_low_t, acts_low_out, out_sem.at[1]),
    )
    for copy in acts_copies:
        copy.start()

    for block in range(WIDTH // 128):
        cols = slice(block * 128, block * 128 + 128)
        high, low = split(acts_t[cols, :].T)
        acts_high[:, cols] = high
        acts_low[:, cols] = low

    for block in range(4):
        cols = pl.ds(block * 512, 512)
        pltpu.make_async_copy(
            decoder.at[0, :, cols], dec.at[:, cols], dec_sem.at[block]
        ).wait()

    @pl.loop(0, WIDTH // 16)
    def _(block):
        rows = pl.ds(block * 16, 16)
        high, low = split(dec[rows, :])
        dec_high[rows, :] = high
        dec_low[rows, :] = low

    def partial(cols):
        high = dec_high[:, cols]
        return (
            jnp.dot(acts_high[...], high, preferred_element_type=F32)
            + jnp.dot(acts_low[...], high, preferred_element_type=F32)
            + jnp.dot(acts_high[...], dec_low[:, cols], preferred_element_type=F32)
        )

    def part_copy(n):
        return pltpu.make_async_remote_copy(
            src_ref=part_send.at[n], dst_ref=part_rx.at[n], send_sem=part_ssem.at[n],
            recv_sem=part_rsem.at[n], device_id=partner, device_id_type=MESH)

    part_send[0] = partial(pl.ds(pl.multiple_of((1 - core) * HALF, 256), 256))
    pl.semaphore_wait(barrier, 30)
    part_copy(0).start()

    @pl.loop(1, PAIRS)
    def _(d):
        map_copy(d).start()

    @pl.loop(1, HALF // 256)
    def _(n):
        part_send[n] = partial(pl.ds(pl.multiple_of((1 - core) * HALF + n * 256, 256), 256))
        part_copy(n).start()

    @pl.loop(0, HALF // 256)
    def _(n):
        part_own[n] = partial(pl.ds(pl.multiple_of(core * HALF + n * 256, 256), 256))

    @pl.loop(0, HALF // 256)
    def _(n):
        part_copy(n).wait_recv()

    def rows_of(q2):
        return pl.ds(pl.multiple_of(q2 * ROWS, ROWS), ROWS)

    def scale_copy(d):
        q2, peer = plane_peer(d)
        return pltpu.make_async_remote_copy(
            src_ref=scale_send.at[q2], dst_ref=scale_rx.at[q], send_sem=scale_ssem.at[q2],
            recv_sem=scale_rsem.at[q], device_id=peer, device_id_type=MESH)

    def scale_arrival(q2):
        return pltpu.make_async_remote_copy(
            src_ref=scale_send.at[q2], dst_ref=scale_rx.at[q2], send_sem=scale_ssem.at[q],
            recv_sem=scale_rsem.at[q2], device_id=partner, device_id_type=MESH)

    def plane_copy(d):
        q2, peer = plane_peer(d)
        return pltpu.make_async_remote_copy(
            src_ref=plane_send.at[q2], dst_ref=plane_rx.at[q], send_sem=plane_ssem.at[q2],
            recv_sem=plane_rsem.at[q], device_id=peer, device_id_type=MESH)

    def plane_arrival(q2):
        return pltpu.make_async_remote_copy(
            src_ref=plane_send.at[q2], dst_ref=plane_rx.at[q2], send_sem=plane_ssem.at[q],
            recv_sem=plane_rsem.at[q2], device_id=partner, device_id_type=MESH)

    def encode(q2):
        rows = rows_of(q2)
        parts = []
        for n in range(HALF // 256):
            x = part_own[n, rows, :] + part_rx[n, rows, :]
            parts += [x[:, :128], x[:, 128:]]
        peak = jnp.abs(parts[0])
        for x in parts[1:]:
            peak = jnp.maximum(peak, jnp.abs(x))
        peak = jnp.maximum(jnp.max(peak, axis=0, keepdims=True), 1e-30)
        inverse = 32000.0 / peak
        codes = [jnp.round(x * inverse).astype(jnp.int16) for x in parts]
        return codes, peak * (1.0 / 32000.0)

    @pl.loop(0, 15)
    def _(d):
        q2 = plane_peer(d)[0]
        codes, scale = encode(q2)
        scale_send[q2] = scale
        for m in range(8):
            plane_send[q2, :, m * 128:m * 128 + 128] = codes[m]
        scale_copy(d).start()
        plane_copy(d).start()

    codes, scale = encode(q)
    scale_rx[q] = scale
    for m in range(8):
        plane_rx[q, :, m * 128:m * 128 + 128] = codes[m]

    @pl.loop(1, PAIRS)
    def _(d):
        map_arrival(d).wait_recv()

    @pl.loop(0, 15)
    def _(d):
        plane_arrival(plane_peer(d)[0]).wait_recv()
        scale_arrival(plane_peer(d)[0]).wait_recv()

    layer_sum[...] = jnp.zeros_like(layer_sum)

    @pl.loop(0, PAIRS)
    def _(p2):
        scales = [jnp.concatenate([scale_rx[2 * p2 + k]] * 8, axis=1) for k in range(2)]
        both = (
            plane_rx[2 * p2].astype(F32) * scales[0] + plane_rx[2 * p2 + 1].astype(F32) * scales[1]
        )
        goal2 = map_rx[p2, 4:5, 0:1]
        for l in range(LAYERS):
            layer_sum[l] += jnp.where(goal2 == l, both, 0.0)

    for l in range(LAYERS):
        for m in range(8):
            line_wide[pl.ds(l * 8 + m, 16, stride=24), :] = layer_sum[l, :, m * 128:m * 128 + 128]

    @pl.loop(0, LINE)
    def _(w2):
        x = line_wide[pl.ds(pl.multiple_of(w2 * 24, 8), 24), :]
        peak = jnp.maximum(jnp.max(jnp.abs(x), axis=0, keepdims=True), 1e-30)
        power = jnp.ceil(jnp.log2(peak * (1.0 / 32000.0)))
        codes = jnp.round(x * jnp.exp2(-power))
        line_send[w2] = jnp.concatenate(
            [codes, jnp.broadcast_to(power, (8, 128))], axis=0).astype(jnp.int16)

    def line_copy(d):
        w2, peer = line_peer(d)
        return pltpu.make_async_remote_copy(
            src_ref=line_send.at[w2], dst_ref=line_rx.at[w], send_sem=line_ssem.at[w2],
            recv_sem=line_rsem.at[w], device_id=peer, device_id_type=MESH)

    def line_arrival(w2):
        return pltpu.make_async_remote_copy(
            src_ref=line_send.at[w2], dst_ref=line_rx.at[w2], send_sem=line_ssem.at[w],
            recv_sem=line_rsem.at[w2], device_id=partner, device_id_type=MESH)

    @pl.loop(0, 15)
    def _(d):
        line_copy(d).start()

    line_rx[w] = line_send[w]

    @pl.loop(0, 15)
    def _(d):
        line_arrival(line_peer(d)[0]).wait_recv()

    for half in range(2):
        total = jnp.zeros((24, 128), F32)
        for z2 in range(8):
            piece = line_rx[2 * z2 + half].astype(F32)
            total = total + piece[0:24] * jnp.exp2(piece[24:25])
        for l in range(LAYERS):
            part = total[l * 8:l * 8 + 8]
            rows = slice(half * 8, half * 8 + 8)
            recon[l, rows, :] = part
            err_send[half, l * 8:l * 8 + 8, :] = (part - target[l, rows, :]).astype(BF16)
        err_send[half, 24:32, :] = jnp.zeros((8, 128), BF16)

    def err_copy(d):
        w2, peer = line_peer(d)
        return pltpu.make_async_remote_copy(
            src_ref=err_send.at[lax.rem(w2, 2)], dst_ref=err_rx.at[w], send_sem=err_ssem.at[w2],
            recv_sem=err_rsem.at[w], device_id=peer, device_id_type=MESH)

    def err_arrival(w2):
        return pltpu.make_async_remote_copy(
            src_ref=err_send.at[0], dst_ref=err_rx.at[w2], send_sem=err_ssem.at[w],
            recv_sem=err_rsem.at[w2], device_id=partner, device_id_type=MESH)

    @pl.loop(0, 15)
    def _(d):
        err_copy(d).start()

    err_rx[w] = err_send[core]

    @pl.loop(0, 15)
    def _(d):
        err_arrival(line_peer(d)[0]).wait_recv()

    @pl.loop(0, LINE)
    def _(w2):
        err_wide[pl.ds(pl.multiple_of(w2 * 32, 32), 32), :] = err_rx[w2].astype(F32)

    for l in range(LAYERS):
        for m in range(8):
            err_layers[l, :, m * 128:m * 128 + 128] = err_wide[pl.ds(l * 8 + m, 16, stride=32), :]

    @pl.loop(0, PAIRS)
    def _(p2):
        goal2 = map_rx[p2, 4:5, 0:1]
        chosen = jnp.zeros((ROWS, HALF), F32)
        for l in range(LAYERS):
            chosen = jnp.where(goal2 == l, err_layers[l], chosen)
        err_pick[p2] = chosen.astype(BF16)

    def spread_copy(d):
        q2, peer = plane_peer(d)
        return pltpu.make_async_remote_copy(
            src_ref=err_pick.at[q2 // 2], dst_ref=err.at[core, rows_of(q)], send_sem=spread_ssem.at[q2],
            recv_sem=spread_rsem.at[q], device_id=peer, device_id_type=MESH)

    def spread_arrival(q2):
        return pltpu.make_async_remote_copy(
            src_ref=err_pick.at[0], dst_ref=err.at[core, rows_of(q2)], send_sem=spread_ssem.at[q],
            recv_sem=spread_rsem.at[q2], device_id=partner, device_id_type=MESH)

    def relay_copy(q2):
        piece = err.at[core, rows_of(q2)]
        return pltpu.make_async_remote_copy(
            src_ref=piece, dst_ref=piece, send_sem=relay_ssem.at[q2],
            recv_sem=relay_rsem.at[q2], device_id=partner, device_id_type=MESH)

    def relay_arrival(q2):
        piece = err.at[1 - core, rows_of(q2)]
        return pltpu.make_async_remote_copy(
            src_ref=piece, dst_ref=piece, send_sem=relay_ssem.at[q2],
            recv_sem=relay_rsem.at[q2], device_id=partner, device_id_type=MESH)

    @pl.loop(0, 15)
    def _(d):
        spread_copy(d).start()

    err[core, rows_of(q), :] = err_pick[p]
    relay_copy(q).start()

    @pl.loop(0, 15)
    def _(d):
        q2 = plane_peer(d)[0]
        spread_arrival(q2).wait_recv()
        relay_copy(q2).start()

    @pl.loop(0, PLANE)
    def _(q2):
        relay_arrival(q2).wait_recv()

    err_copy_out = pltpu.make_async_copy(err, error_out, out_sem.at[2])
    err_copy_out.start()

    @pl.loop(0, WIDTH // 128)
    def _(n):
        rows = pl.ds(pl.multiple_of(n * 128, 128), 128)
        total = jnp.zeros((TOK, 128), F32)
        for half in range(2):
            cols = slice(half * HALF, half * HALF + HALF)
            total = total + nt(err[half], dec_high[rows, cols]) + nt(err[half], dec_low[rows, cols])
        back[n] = total

    local = indices[layer] - f * WIDTH
    lane = jnp.bitwise_and(local, 127)
    block_of = jnp.right_shift(local, 7)
    found = jnp.zeros((TOK, ACTIVE), F32)
    for n in range(WIDTH // 128):
        here = jnp.take_along_axis(back[n], lane, axis=1)
        found = jnp.where(block_of == n, here, found)
    picked[...] = found

    def pick_copy(d):
        q2, peer = plane_peer(d)
        return pltpu.make_async_remote_copy(
            src_ref=picked.at[rows_of(q2)], dst_ref=pick_rx.at[q], send_sem=pick_ssem.at[q2],
            recv_sem=pick_rsem.at[q], device_id=peer, device_id_type=MESH)

    def pick_arrival(q2):
        return pltpu.make_async_remote_copy(
            src_ref=picked.at[rows_of(q2)], dst_ref=pick_rx.at[q2], send_sem=pick_ssem.at[q],
            recv_sem=pick_rsem.at[q2], device_id=partner, device_id_type=MESH)

    @pl.loop(0, 15)
    def _(d):
        pick_copy(d).start()

    pick_rx[q] = picked[rows_of(q), :]
    pick_line[...] = jnp.zeros_like(pick_line)

    @pl.loop(0, 15)
    def _(d):
        pick_arrival(plane_peer(d)[0]).wait_recv()

    sums = [jnp.zeros((ROWS, ACTIVE), F32) for _ in range(LAYERS)]
    for p2 in range(PAIRS):
        both = pick_rx[2 * p2] + pick_rx[2 * p2 + 1]
        source2 = map_rx[p2, 0:1, 0:1]
        for l in range(LAYERS):
            sums[l] = sums[l] + jnp.where(source2 == l, both, 0.0)
    for l in range(LAYERS):
        pick_line[pl.ds(l, 16, stride=8), :] = sums[l]

    def feat_copy(d):
        w2, peer = line_peer(d)
        return pltpu.make_async_remote_copy(
            src_ref=pick_line.at[pl.ds(pl.multiple_of(w2 * 8, 8), 8)], dst_ref=feat_rx.at[w],
            send_sem=feat_ssem.at[w2], recv_sem=feat_rsem.at[w], device_id=peer, device_id_type=MESH)

    def feat_arrival(w2):
        return pltpu.make_async_remote_copy(
            src_ref=pick_line.at[pl.ds(0, 8)], dst_ref=feat_rx.at[w2],
            send_sem=feat_ssem.at[w], recv_sem=feat_rsem.at[w2], device_id=partner, device_id_type=MESH)

    @pl.loop(0, 15)
    def _(d):
        feat_copy(d).start()

    feat_rx[w] = pick_line[pl.ds(pl.multiple_of(w * 8, 8), 8), :]

    @pl.loop(0, 15)
    def _(d):
        feat_arrival(line_peer(d)[0]).wait_recv()

    total = feat_rx[0]
    for w2 in range(1, LINE):
        total = total + feat_rx[w2]
    feat[...] = total[0:LAYERS]
    for copy in acts_copies + (err_copy_out,):
        copy.wait()

    @pl.loop(1, PAIRS)
    def _(d):
        map_copy(d).wait_send()

    @pl.loop(0, 15)
    def _(d):
        scale_copy(d).wait_send()
        plane_copy(d).wait_send()
        line_copy(d).wait_send()
        err_copy(d).wait_send()
        spread_copy(d).wait_send()
        pick_copy(d).wait_send()
        feat_copy(d).wait_send()

    @pl.loop(0, HALF // 256)
    def _(n):
        part_copy(n).wait_send()

    @pl.loop(0, PLANE)
    def _(q2):
        relay_copy(q2).wait_send()


def grad_kernel(acts_high_t, acts_low_t, err, recon, feat, out, recon_out, feat_out):
    e = err[0]
    out[...] = (
        jnp.dot(acts_high_t[...], e, preferred_element_type=F32)
        + jnp.dot(acts_low_t[...], e, preferred_element_type=F32)
    )
    for k in range(16):
        recon_out[:, k * 128:k * 128 + 128] = recon[:, k, :].astype(BF16)
    for l in range(LAYERS):
        feat_out[l] = feat[l:l + 1, :]


def body(decoder, pair_map, indices, values, target):
    vmem = pl.BlockSpec(memory_space=pltpu.VMEM)
    dma = pltpu.SemaphoreType.DMA
    recon, feat, err, acts_high_t, acts_low_t = pl.pallas_call(
        exchange_kernel,
        out_shape=(
            jax.ShapeDtypeStruct((LAYERS, 16, 128), F32),
            jax.ShapeDtypeStruct((LAYERS, ACTIVE), F32),
            jax.ShapeDtypeStruct((2, TOK, HALF), BF16),
            jax.ShapeDtypeStruct((WIDTH, TOK), BF16),
            jax.ShapeDtypeStruct((WIDTH, TOK), BF16),
        ),
        in_specs=[pl.BlockSpec(memory_space=pltpu.SMEM), vmem, vmem, vmem, pl.BlockSpec(memory_space=pl.ANY)],
        out_specs=(vmem, vmem) + (pl.BlockSpec(memory_space=pl.ANY),) * 3,
        scratch_shapes=[
            pltpu.VMEM((WIDTH, TOK), BF16),
            pltpu.VMEM((WIDTH, TOK), BF16),
            pltpu.VMEM((WIDTH, MODEL), F32),
            pltpu.VMEM((WIDTH, MODEL), BF16),
            pltpu.VMEM((WIDTH, MODEL), BF16),
            pltpu.VMEM((ACTIVE, TOK), jnp.int32),
            pltpu.VMEM((ACTIVE, TOK), F32),
            pltpu.VMEM((WIDTH, TOK), F32),
            pltpu.VMEM((TOK, WIDTH), BF16),
            pltpu.VMEM((TOK, WIDTH), BF16),
            pltpu.VMEM((8, 128), jnp.int32),
            pltpu.VMEM((PAIRS, 8, 128), jnp.int32),
            pltpu.VMEM((HALF // 256, TOK, 256), F32),
            pltpu.VMEM((HALF // 256, TOK, 256), F32),
            pltpu.VMEM((HALF // 256, TOK, 256), F32),
            pltpu.VMEM((PLANE, 1, 128), F32),
            pltpu.VMEM((PLANE, 1, 128), F32),
            pltpu.VMEM((PLANE, ROWS, HALF), jnp.int16),
            pltpu.VMEM((PLANE, ROWS, HALF), jnp.int16),
            pltpu.VMEM((LAYERS, ROWS, HALF), F32),
            pltpu.VMEM((LINE * 24, 128), F32),
            pltpu.VMEM((LINE, 32, 128), jnp.int16),
            pltpu.VMEM((LINE, 32, 128), jnp.int16),
            pltpu.VMEM((2, 32, 128), BF16),
            pltpu.VMEM((LINE, 32, 128), BF16),
            pltpu.VMEM((LINE * 32, 128), F32),
            pltpu.VMEM((LAYERS, ROWS, HALF), F32),
            pltpu.VMEM((PAIRS, ROWS, HALF), BF16),
            pltpu.VMEM((2, TOK, HALF), BF16),
            pltpu.VMEM((WIDTH // 128, TOK, 128), F32),
            pltpu.VMEM((TOK, ACTIVE), F32),
            pltpu.VMEM((PLANE, ROWS, ACTIVE), F32),
            pltpu.VMEM((LINE * 8, 128), F32),
            pltpu.VMEM((LINE, 8, 128), F32),
            dma((4,)), dma((3,)),
            dma((PAIRS,)), dma((PAIRS,)),
            dma((4,)), dma((4,)),
            dma((PLANE,)), dma((PLANE,)),
            dma((PLANE,)), dma((PLANE,)),
            dma((LINE,)), dma((LINE,)),
            dma((LINE,)), dma((LINE,)),
            dma((PLANE,)), dma((PLANE,)),
            dma((PLANE,)), dma((PLANE,)),
            dma((PLANE,)), dma((PLANE,)),
            dma((LINE,)), dma((LINE,)),
        ],
        compiler_params=pltpu.CompilerParams(
            collective_id=0, has_side_effects=True, vmem_limit_bytes=56 * 2**20
        ),
    )(pair_map, indices, values, target.reshape(LAYERS, 16, 128), decoder)
    dec_grad, recon, feat = pl.pallas_call(
        grad_kernel,
        grid=(2,),
        out_shape=(
            jax.ShapeDtypeStruct((WIDTH, MODEL), F32),
            jax.ShapeDtypeStruct((LAYERS, MODEL), BF16),
            jax.ShapeDtypeStruct((LAYERS, 1, ACTIVE), F32),
        ),
        in_specs=[
            pl.BlockSpec((WIDTH, TOK), lambda n: (0, 0)),
            pl.BlockSpec((WIDTH, TOK), lambda n: (0, 0)),
            pl.BlockSpec((1, TOK, HALF), lambda n: (n, 0, 0)),
            pl.BlockSpec((LAYERS, 16, 128), lambda n: (0, 0, 0)),
            pl.BlockSpec((LAYERS, ACTIVE), lambda n: (0, 0)),
        ],
        out_specs=(
            pl.BlockSpec((WIDTH, HALF), lambda n: (0, n)),
            pl.BlockSpec((LAYERS, MODEL), lambda n: (0, 0)),
            pl.BlockSpec((LAYERS, 1, ACTIVE), lambda n: (0, 0, 0)),
        ),
    )(acts_high_t, acts_low_t, err, recon, feat)
    return recon.reshape(LAYERS, 1, MODEL), dec_grad.reshape(1, WIDTH, MODEL), feat


def solution(mesh):
    in_specs = (P("pair", "feat", None), P("pair", None), P(), P(), P(None, ("pair", "feat"), None))
    out_specs = (
        P(None, ("pair", "feat"), None),
        P("pair", "feat", None),
        P(None, ("pair", "feat"), None),
    )
    return jax.shard_map(body, mesh=mesh, in_specs=in_specs, out_specs=out_specs, check_vma=False)
```

```python
import jax
import jax.numpy as jnp
from jax import lax
from jax.experimental import pallas as pl
from jax.experimental.pallas import tpu as pltpu
from jax.sharding import PartitionSpec as P

MESH = pl.DeviceIdType.MESH
F32 = jnp.float32
BF16 = jnp.bfloat16

LAYERS = 3
TOK = 256
ACTIVE = 128
WIDTH = 512
MODEL = 2048
HALF = MODEL // 2
PAIRS = 8
PLANE = 16
LINE = 16
ROWS = TOK // PLANE


def split(x):
    high = x.astype(BF16)
    return high, (x - high.astype(F32)).astype(BF16)


def nt(a, b):
    return lax.dot_general(a, b, (((1,), (1,)), ((), ())), preferred_element_type=F32)


def exchange_kernel(
    pair_map, indices, values, target, decoder,
    recon, feat, error_out, acts_high_out, acts_low_out,
    acts_high_t, acts_low_t, dec, dec_high, dec_low, ids_t, vals_t, acts,
    map_send, map_rx, part_send, part_rx, part_own, scale_send, scale_rx, plane_send, plane_rx, layer_sum,
    line_wide,
    line_send, line_rx, err_send, err_rx, err_wide, err_layers, err_pick, err,
    picked, pick_rx, pick_wide, pick_line, feat_rx,
    dec_sem, out_sem, map_ssem, map_rsem, part_ssem, part_rsem, scale_ssem, scale_rsem, plane_ssem, plane_rsem,
    line_ssem, line_rsem, err_ssem, err_rsem, spread_ssem, spread_rsem,
    relay_ssem, relay_rsem, pick_ssem, pick_rsem, feat_ssem, feat_rsem,
):
    p = lax.axis_index("pair")
    f = lax.axis_index("feat")
    y = f // 16
    w = lax.rem(f, 16)
    core = lax.rem(f, 2)
    q = p * 2 + y

    def plane_peer(i):
        same, a, b = i // 8, lax.rem(i, 8) // 2, lax.rem(i, 2)
        far = 2 + jnp.where(a == 1, 3, jnp.where(a == 2, 1, jnp.where(a == 3, 2, 0)))
        x2 = lax.rem(lax.rem(p, 4) + far, 4)
        low2 = lax.rem(p // 4 + 1 - same, 2)
        y2 = lax.rem(y + 1 - b, 2)
        p2 = low2 * 4 + x2
        return p2 * 2 + y2, (p2, y2 * 16 + w)

    def line_peer(i):
        a, b = i // 2, lax.rem(i, 2)
        far = 4 + jnp.where(lax.rem(a, 2) == 1, 8 - (a + 1) // 2, a // 2)
        w2 = lax.rem(w // 2 + far, 8) * 2 + lax.rem(core + 1 - b, 2)
        return w2, (p, y * 16 + w2)

    partner = (p, f + 1 - 2 * core)

    for block in range(4):
        cols = pl.ds(block * 512, 512)
        pltpu.make_async_copy(
            decoder.at[0, :, cols], dec.at[:, cols], dec_sem.at[block]
        ).start()

    barrier = pltpu.get_barrier_semaphore()

    @pl.loop(0, 15)
    def _(d):
        pl.semaphore_signal(barrier, inc=1, device_id=plane_peer(d)[1], device_id_type=MESH)
        pl.semaphore_signal(barrier, inc=1, device_id=line_peer(d)[1], device_id_type=MESH)

    source = pair_map[0, 0]
    goal = pair_map[0, 1]
    row = lax.broadcasted_iota(jnp.int32, (8, 128), 0)
    tile = jnp.where(row < 4, source, goal)
    map_send[...] = tile
    map_rx[p] = tile

    def map_copy(d):
        p2 = lax.rem(p + d, PAIRS)
        return pltpu.make_async_remote_copy(
            src_ref=map_send, dst_ref=map_rx.at[p], send_sem=map_ssem.at[p2],
            recv_sem=map_rsem.at[p], device_id=(p2, f), device_id_type=MESH)

    def map_arrival(d):
        p2 = lax.rem(p + d, PAIRS)
        return pltpu.make_async_remote_copy(
            src_ref=map_send, dst_ref=map_rx.at[p2], send_sem=map_ssem.at[p],
            recv_sem=map_rsem.at[p2], device_id=(p2, f), device_id_type=MESH)

    layer = jnp.minimum(source, LAYERS - 1)
    local = indices[layer] - f * WIDTH
    for k in range(2):
        ids_t[k] = local[k * 128:k * 128 + 128].T
        vals_t[k] = values[layer, k * 128:k * 128 + 128, :].T

    def rows_of(q2):
        return pl.ds(pl.multiple_of(q2 * ROWS, ROWS), ROWS)

    def scale_copy(d):
        q2, peer = plane_peer(d)
        return pltpu.make_async_remote_copy(
            src_ref=scale_send.at[q2], dst_ref=scale_rx.at[q], send_sem=scale_ssem.at[q2],
            recv_sem=scale_rsem.at[q], device_id=peer, device_id_type=MESH)

    def scale_arrival(q2):
        return pltpu.make_async_remote_copy(
            src_ref=scale_send.at[q2], dst_ref=scale_rx.at[q2], send_sem=scale_ssem.at[q],
            recv_sem=scale_rsem.at[q2], device_id=partner, device_id_type=MESH)

    def plane_copy(d):
        q2, peer = plane_peer(d)
        return pltpu.make_async_remote_copy(
            src_ref=plane_send.at[q2], dst_ref=plane_rx.at[q], send_sem=plane_ssem.at[q2],
            recv_sem=plane_rsem.at[q], device_id=peer, device_id_type=MESH)

    def plane_arrival(q2):
        return pltpu.make_async_remote_copy(
            src_ref=plane_send.at[q2], dst_ref=plane_rx.at[q2], send_sem=plane_ssem.at[q],
            recv_sem=plane_rsem.at[q2], device_id=partner, device_id_type=MESH)

    def encode(q2):
        rows = rows_of(q2)
        parts = []
        for n in range(HALF // 256):
            x = part_own[n, rows, :] + part_rx[n, rows, :]
            parts += [x[:, :128], x[:, 128:]]
        peak = jnp.abs(parts[0])
        for x in parts[1:]:
            peak = jnp.maximum(peak, jnp.abs(x))
        peak = jnp.maximum(jnp.max(peak, axis=0, keepdims=True), 1e-30)
        inverse = 32000.0 / peak
        codes = [jnp.round(x * inverse).astype(jnp.int16) for x in parts]
        return codes, peak * (1.0 / 32000.0)

    def partial(cols):
        both = jnp.dot(acts[...], dec_high[:, cols], preferred_element_type=F32)
        rest = jnp.dot(acts[0:TOK // 2, :], dec_low[:, cols], preferred_element_type=F32)
        return both[0:TOK // 2] + both[TOK // 2:] + rest

    def tokens_of(same):
        low2 = p // 4 + (1 - 2 * (p // 4)) * (1 - same)
        return low2, pl.ds(pl.multiple_of(low2 * 128, 128), 128)

    def part_copy(same, n):
        tokens = tokens_of(same)[1]
        return pltpu.make_async_remote_copy(
            src_ref=part_send.at[n, tokens], dst_ref=part_rx.at[n, tokens],
            send_sem=part_ssem.at[same * 4 + n], recv_sem=part_rsem.at[same * 4 + n],
            device_id=partner, device_id_type=MESH)

    for same in range(2):
        low2, tokens = tokens_of(same)

        @pl.loop(0, WIDTH // 128)
        def _(block):
            base = pl.multiple_of(block * 128, 128)
            features = lax.broadcasted_iota(jnp.int32, (128, 128), 0) + base

            def step(k, total):
                for j in range(4):
                    ids = ids_t[low2, pl.ds(k * 4 + j, 1), :]
                    vals = vals_t[low2, pl.ds(k * 4 + j, 1), :]
                    total = jnp.where(ids == features, vals, total)
                return total

            total = lax.fori_loop(0, ACTIVE // 4, step, jnp.zeros((128, 128), F32))
            high, low = split(total)
            acts_high_t[pl.ds(base, 128), tokens] = high
            acts_low_t[pl.ds(base, 128), tokens] = low
            high, low = split(total.T)
            cols = pl.ds(pl.multiple_of(base, 128), 128)
            acts[0:TOK // 2, cols] = high
            acts[TOK // 2:, cols] = low

        if same == 0:
            for block in range(4):
                cols = pl.ds(block * 512, 512)
                pltpu.make_async_copy(
                    decoder.at[0, :, cols], dec.at[:, cols], dec_sem.at[block]
                ).wait()

            @pl.loop(0, WIDTH // 16)
            def _(block):
                rows = pl.ds(block * 16, 16)
                high, low = split(dec[rows, :])
                dec_high[rows, :] = high
                dec_low[rows, :] = low

            part_send[0, tokens, :] = partial(pl.ds(pl.multiple_of((1 - core) * HALF, 256), 256))
            pl.semaphore_wait(barrier, 30)
            part_copy(0, 0).start()

            @pl.loop(1, PAIRS)
            def _(d):
                map_copy(d).start()

        @pl.loop(1 - same, HALF // 256)
        def _(n):
            part_send[n, tokens, :] = partial(pl.ds(pl.multiple_of((1 - core) * HALF + n * 256, 256), 256))
            part_copy(same, n).start()

        @pl.loop(0, HALF // 256)
        def _(n):
            part_own[n, tokens, :] = partial(pl.ds(pl.multiple_of(core * HALF + n * 256, 256), 256))

        @pl.loop(0, HALF // 256)
        def _(n):
            part_copy(same, n).wait_recv()

        @pl.loop(8 * same, 8 + 7 * same)
        def _(d):
            q2 = plane_peer(d)[0]
            codes, scale = encode(q2)
            scale_send[q2] = scale
            for m in range(8):
                plane_send[q2, :, m * 128:m * 128 + 128] = codes[m]
            scale_copy(d).start()
            plane_copy(d).start()

    acts_copies = (
        pltpu.make_async_copy(acts_high_t, acts_high_out, out_sem.at[0]),
        pltpu.make_async_copy(acts_low_t, acts_low_out, out_sem.at[1]),
    )
    for copy in acts_copies:
        copy.start()

    codes, scale = encode(q)
    scale_rx[q] = scale
    for m in range(8):
        plane_rx[q, :, m * 128:m * 128 + 128] = codes[m]

    @pl.loop(1, PAIRS)
    def _(d):
        map_arrival(d).wait_recv()

    layer_sum[...] = jnp.zeros_like(layer_sum)

    def add_pair(q2, q3):
        scales = [jnp.concatenate([scale_rx[k]] * 8, axis=1) for k in (q2, q3)]
        both = plane_rx[q2].astype(F32) * scales[0] + plane_rx[q3].astype(F32) * scales[1]
        goal2 = map_rx[q2 // 2, 4:5, 0:1]
        for l in range(LAYERS):
            layer_sum[l] += jnp.where(goal2 == l, both, 0.0)

    def wait_plane(q2):
        plane_arrival(q2).wait_recv()
        scale_arrival(q2).wait_recv()

    @pl.loop(0, 7)
    def _(j):
        q2, q3 = plane_peer(2 * j)[0], plane_peer(2 * j + 1)[0]
        wait_plane(q2)
        wait_plane(q3)
        add_pair(q2, q3)

    q2 = plane_peer(14)[0]
    wait_plane(q2)
    add_pair(q2, q)

    tiles = [(l, m, layer_sum[l, :, m * 128:m * 128 + 128]) for l in range(LAYERS) for m in range(8)]
    peak = jnp.full((ROWS, 128), 1e-30, F32)
    for _, _, x in tiles:
        peak = jnp.maximum(peak, jnp.abs(x))
    power = jnp.ceil(jnp.log2(peak * (1.0 / 32000.0)))
    inverse = jnp.exp2(-power)
    for l, m, x in tiles:
        line_wide[pl.ds(l * 8 + m, 16, stride=32), :] = jnp.round(x * inverse)
    for m in range(8):
        line_wide[pl.ds(24 + m, 16, stride=32), :] = power
    for w2 in range(LINE):
        line_send[w2] = line_wide[w2 * 32:w2 * 32 + 32, :].astype(jnp.int16)

    def line_copy(d):
        w2, peer = line_peer(d)
        return pltpu.make_async_remote_copy(
            src_ref=line_send.at[w2], dst_ref=line_rx.at[w], send_sem=line_ssem.at[w2],
            recv_sem=line_rsem.at[w], device_id=peer, device_id_type=MESH)

    def line_arrival(w2):
        return pltpu.make_async_remote_copy(
            src_ref=line_send.at[w2], dst_ref=line_rx.at[w2], send_sem=line_ssem.at[w],
            recv_sem=line_rsem.at[w2], device_id=partner, device_id_type=MESH)

    @pl.loop(0, 15)
    def _(d):
        line_copy(d).start()

    line_rx[w] = line_send[w]

    @pl.loop(0, 15)
    def _(d):
        line_arrival(line_peer(d)[0]).wait_recv()

    for half in range(2):
        total = jnp.zeros((24, 128), F32)
        for z2 in range(8):
            piece = line_rx[2 * z2 + half].astype(F32)
            total = total + piece[0:24] * jnp.exp2(piece[24:25])
        for l in range(LAYERS):
            part = total[l * 8:l * 8 + 8]
            rows = slice(half * 8, half * 8 + 8)
            recon[l, rows, :] = part
            err_send[half, l * 8:l * 8 + 8, :] = (part - target[l, rows, :]).astype(BF16)

    def err_copy(d):
        w2, peer = line_peer(d)
        return pltpu.make_async_remote_copy(
            src_ref=err_send.at[lax.rem(w2, 2)], dst_ref=err_rx.at[w], send_sem=err_ssem.at[w2],
            recv_sem=err_rsem.at[w], device_id=peer, device_id_type=MESH)

    def err_arrival(w2):
        return pltpu.make_async_remote_copy(
            src_ref=err_send.at[0], dst_ref=err_rx.at[w2], send_sem=err_ssem.at[w],
            recv_sem=err_rsem.at[w2], device_id=partner, device_id_type=MESH)

    @pl.loop(0, 15)
    def _(d):
        err_copy(d).start()

    err_rx[w] = err_send[core]

    @pl.loop(0, 15)
    def _(d):
        err_arrival(line_peer(d)[0]).wait_recv()

    @pl.loop(0, LINE)
    def _(w2):
        err_wide[pl.ds(pl.multiple_of(w2 * 24, 8), 24), :] = err_rx[w2].astype(F32)

    for l in range(LAYERS):
        for m in range(8):
            err_layers[l, :, m * 128:m * 128 + 128] = err_wide[pl.ds(l * 8 + m, 16, stride=24), :]

    def spread_copy(d):
        q2, peer = plane_peer(d)
        return pltpu.make_async_remote_copy(
            src_ref=err_pick.at[q2 // 2], dst_ref=err.at[core, rows_of(q)], send_sem=spread_ssem.at[q2],
            recv_sem=spread_rsem.at[q], device_id=peer, device_id_type=MESH)

    def spread_arrival(q2):
        return pltpu.make_async_remote_copy(
            src_ref=err_pick.at[0], dst_ref=err.at[core, rows_of(q2)], send_sem=spread_ssem.at[q],
            recv_sem=spread_rsem.at[q2], device_id=partner, device_id_type=MESH)

    def relay_copy(q2):
        piece = err.at[core, rows_of(q2)]
        return pltpu.make_async_remote_copy(
            src_ref=piece, dst_ref=piece, send_sem=relay_ssem.at[q2],
            recv_sem=relay_rsem.at[q2], device_id=partner, device_id_type=MESH)

    def relay_arrival(q2):
        piece = err.at[1 - core, rows_of(q2)]
        return pltpu.make_async_remote_copy(
            src_ref=piece, dst_ref=piece, send_sem=relay_ssem.at[q2],
            recv_sem=relay_rsem.at[q2], device_id=partner, device_id_type=MESH)

    def choose(p2):
        goal2 = map_rx[p2, 4:5, 0:1]
        chosen = jnp.zeros((ROWS, HALF), F32)
        for l in range(LAYERS):
            chosen = jnp.where(goal2 == l, err_layers[l], chosen)
        err_pick[p2] = chosen.astype(BF16)

    @pl.loop(0, 7)
    def _(j):
        choose(plane_peer(2 * j)[0] // 2)
        spread_copy(2 * j).start()
        spread_copy(2 * j + 1).start()

    choose(p)
    spread_copy(14).start()
    err[core, rows_of(q), :] = err_pick[p]
    relay_copy(q).start()

    def pick_copy(d):
        q2, peer = plane_peer(d)
        return pltpu.make_async_remote_copy(
            src_ref=picked.at[rows_of(q2)], dst_ref=pick_rx.at[q], send_sem=pick_ssem.at[q2],
            recv_sem=pick_rsem.at[q], device_id=peer, device_id_type=MESH)

    def pick_arrival(q2):
        return pltpu.make_async_remote_copy(
            src_ref=picked.at[rows_of(q2)], dst_ref=pick_rx.at[q2], send_sem=pick_ssem.at[q],
            recv_sem=pick_rsem.at[q2], device_id=partner, device_id_type=MESH)

    for same in range(2):
        last = 8 + 7 * same
        low2, tokens = tokens_of(same)

        @pl.loop(8 * same, last)
        def _(d):
            q2 = plane_peer(d)[0]
            spread_arrival(q2).wait_recv()
            relay_copy(q2).start()

        @pl.loop(0, 8)
        def _(k):
            relay_arrival(low2 * 8 + k).wait_recv()

        local = indices[layer, tokens, :] - f * WIDTH
        lane = jnp.bitwise_and(local, 127)
        block_of = jnp.right_shift(local, 7)
        found = jnp.zeros((TOK // 2, ACTIVE), F32)
        for n in range(WIDTH // 256):
            rows = slice(n * 256, n * 256 + 256)
            back = jnp.zeros((TOK // 2, 256), F32)
            for half in range(2):
                cols = slice(half * HALF, half * HALF + HALF)
                e = err[half, tokens, :]
                back = back + nt(e, dec_high[rows, cols]) + nt(e, dec_low[rows, cols])
            for k in range(2):
                here = jnp.take_along_axis(back[:, k * 128:k * 128 + 128], lane, axis=1)
                found = jnp.where(block_of == 2 * n + k, here, found)
        picked[tokens, :] = found

        @pl.loop(8 * same, last)
        def _(d):
            pick_copy(d).start()

    err_copy_out = pltpu.make_async_copy(err, error_out, out_sem.at[2])
    err_copy_out.start()
    pick_rx[q] = picked[rows_of(q), :]
    pick_wide[...] = jnp.zeros_like(pick_wide)

    @pl.loop(0, 15)
    def _(d):
        pick_arrival(plane_peer(d)[0]).wait_recv()

    sums = [jnp.zeros((ROWS, ACTIVE), F32) for _ in range(LAYERS)]
    for p2 in range(PAIRS):
        both = pick_rx[2 * p2] + pick_rx[2 * p2 + 1]
        source2 = map_rx[p2, 0:1, 0:1]
        for l in range(LAYERS):
            sums[l] = sums[l] + jnp.where(source2 == l, both, 0.0)
    for l in range(LAYERS):
        pick_wide[pl.ds(l, 16, stride=8), :] = sums[l]

    for w2 in range(LINE):
        pick_line[w2] = pick_wide[w2 * 8:w2 * 8 + 4, :]

    def feat_copy(d):
        w2, peer = line_peer(d)
        return pltpu.make_async_remote_copy(
            src_ref=pick_line.at[w2], dst_ref=feat_rx.at[w],
            send_sem=feat_ssem.at[w2], recv_sem=feat_rsem.at[w], device_id=peer, device_id_type=MESH)

    def feat_arrival(w2):
        return pltpu.make_async_remote_copy(
            src_ref=pick_line.at[w2], dst_ref=feat_rx.at[w2],
            send_sem=feat_ssem.at[w], recv_sem=feat_rsem.at[w2], device_id=partner, device_id_type=MESH)

    @pl.loop(0, 15)
    def _(d):
        feat_copy(d).start()

    feat_rx[w] = pick_line[w]

    @pl.loop(0, 15)
    def _(d):
        feat_arrival(line_peer(d)[0]).wait_recv()

    total = feat_rx[0]
    for w2 in range(1, LINE):
        total = total + feat_rx[w2]
    feat[...] = total[0:LAYERS]
    for copy in acts_copies + (err_copy_out,):
        copy.wait()

    @pl.loop(1, PAIRS)
    def _(d):
        map_copy(d).wait_send()

    @pl.loop(0, 15)
    def _(d):
        scale_copy(d).wait_send()
        plane_copy(d).wait_send()
        line_copy(d).wait_send()
        err_copy(d).wait_send()
        spread_copy(d).wait_send()
        pick_copy(d).wait_send()
        feat_copy(d).wait_send()

    @pl.loop(0, HALF // 256)
    def _(n):
        part_copy(0, n).wait_send()
        part_copy(1, n).wait_send()

    @pl.loop(0, PLANE)
    def _(q2):
        relay_copy(q2).wait_send()


def grad_kernel(acts_high_t, acts_low_t, err, recon, feat, out, recon_out, feat_out):
    e = err[0]
    out[...] = (
        jnp.dot(acts_high_t[...], e, preferred_element_type=F32)
        + jnp.dot(acts_low_t[...], e, preferred_element_type=F32)
    )
    for k in range(16):
        recon_out[:, k * 128:k * 128 + 128] = recon[:, k, :].astype(BF16)
    for l in range(LAYERS):
        feat_out[l] = feat[l:l + 1, :]


def body(decoder, pair_map, indices, values, target):
    vmem = pl.BlockSpec(memory_space=pltpu.VMEM)
    dma = pltpu.SemaphoreType.DMA
    recon, feat, err, acts_high_t, acts_low_t = pl.pallas_call(
        exchange_kernel,
        out_shape=(
            jax.ShapeDtypeStruct((LAYERS, 16, 128), F32),
            jax.ShapeDtypeStruct((LAYERS, ACTIVE), F32),
            jax.ShapeDtypeStruct((2, TOK, HALF), BF16),
            jax.ShapeDtypeStruct((WIDTH, TOK), BF16),
            jax.ShapeDtypeStruct((WIDTH, TOK), BF16),
        ),
        in_specs=[pl.BlockSpec(memory_space=pltpu.SMEM), vmem, vmem, vmem, pl.BlockSpec(memory_space=pl.ANY)],
        out_specs=(vmem, vmem) + (pl.BlockSpec(memory_space=pl.ANY),) * 3,
        scratch_shapes=[
            pltpu.VMEM((WIDTH, TOK), BF16),
            pltpu.VMEM((WIDTH, TOK), BF16),
            pltpu.VMEM((WIDTH, MODEL), F32),
            pltpu.VMEM((WIDTH, MODEL), BF16),
            pltpu.VMEM((WIDTH, MODEL), BF16),
            pltpu.VMEM((2, ACTIVE, TOK // 2), jnp.int32),
            pltpu.VMEM((2, ACTIVE, TOK // 2), F32),
            pltpu.VMEM((TOK, WIDTH), BF16),
            pltpu.VMEM((8, 128), jnp.int32),
            pltpu.VMEM((PAIRS, 8, 128), jnp.int32),
            pltpu.VMEM((HALF // 256, TOK, 256), F32),
            pltpu.VMEM((HALF // 256, TOK, 256), F32),
            pltpu.VMEM((HALF // 256, TOK, 256), F32),
            pltpu.VMEM((PLANE, 1, 128), F32),
            pltpu.VMEM((PLANE, 1, 128), F32),
            pltpu.VMEM((PLANE, ROWS, HALF), jnp.int16),
            pltpu.VMEM((PLANE, ROWS, HALF), jnp.int16),
            pltpu.VMEM((LAYERS, ROWS, HALF), F32),
            pltpu.VMEM((LINE * 32, 128), F32),
            pltpu.VMEM((LINE, 32, 128), jnp.int16),
            pltpu.VMEM((LINE, 32, 128), jnp.int16),
            pltpu.VMEM((2, 24, 128), BF16),
            pltpu.VMEM((LINE, 24, 128), BF16),
            pltpu.VMEM((LINE * 24, 128), F32),
            pltpu.VMEM((LAYERS, ROWS, HALF), F32),
            pltpu.VMEM((PAIRS, ROWS, HALF), BF16),
            pltpu.VMEM((2, TOK, HALF), BF16),
            pltpu.VMEM((TOK, ACTIVE), F32),
            pltpu.VMEM((PLANE, ROWS, ACTIVE), F32),
            pltpu.VMEM((LINE * 8, 128), F32),
            pltpu.VMEM((LINE, 4, 128), F32),
            pltpu.VMEM((LINE, 4, 128), F32),
            dma((4,)), dma((3,)),
            dma((PAIRS,)), dma((PAIRS,)),
            dma((8,)), dma((8,)),
            dma((PLANE,)), dma((PLANE,)),
            dma((PLANE,)), dma((PLANE,)),
            dma((LINE,)), dma((LINE,)),
            dma((LINE,)), dma((LINE,)),
            dma((PLANE,)), dma((PLANE,)),
            dma((PLANE,)), dma((PLANE,)),
            dma((PLANE,)), dma((PLANE,)),
            dma((LINE,)), dma((LINE,)),
        ],
        compiler_params=pltpu.CompilerParams(
            collective_id=0, has_side_effects=True, vmem_limit_bytes=56 * 2**20
        ),
    )(pair_map, indices, values, target.reshape(LAYERS, 16, 128), decoder)
    dec_grad, recon, feat = pl.pallas_call(
        grad_kernel,
        grid=(2,),
        out_shape=(
            jax.ShapeDtypeStruct((WIDTH, MODEL), F32),
            jax.ShapeDtypeStruct((LAYERS, MODEL), BF16),
            jax.ShapeDtypeStruct((LAYERS, 1, ACTIVE), F32),
        ),
        in_specs=[
            pl.BlockSpec((WIDTH, TOK), lambda n: (0, 0)),
            pl.BlockSpec((WIDTH, TOK), lambda n: (0, 0)),
            pl.BlockSpec((1, TOK, HALF), lambda n: (n, 0, 0)),
            pl.BlockSpec((LAYERS, 16, 128), lambda n: (0, 0, 0)),
            pl.BlockSpec((LAYERS, ACTIVE), lambda n: (0, 0)),
        ],
        out_specs=(
            pl.BlockSpec((WIDTH, HALF), lambda n: (0, n)),
            pl.BlockSpec((LAYERS, MODEL), lambda n: (0, 0)),
            pl.BlockSpec((LAYERS, 1, ACTIVE), lambda n: (0, 0, 0)),
        ),
    )(acts_high_t, acts_low_t, err, recon, feat)
    return recon.reshape(LAYERS, 1, MODEL), dec_grad.reshape(1, WIDTH, MODEL), feat


def solution(mesh):
    in_specs = (P("pair", "feat", None), P("pair", None), P(), P(), P(None, ("pair", "feat"), None))
    out_specs = (
        P(None, ("pair", "feat"), None),
        P("pair", "feat", None),
        P(None, ("pair", "feat"), None),
    )
    return jax.shard_map(body, mesh=mesh, in_specs=in_specs, out_specs=out_specs, check_vma=False)
```

```python
import jax
import jax.numpy as jnp
from jax import lax
from jax.experimental import pallas as pl
from jax.experimental.pallas import tpu as pltpu
from jax.sharding import PartitionSpec as P

MESH = pl.DeviceIdType.MESH
F32 = jnp.float32
BF16 = jnp.bfloat16

LAYERS = 3
TOK = 256
ACTIVE = 128
WIDTH = 512
MODEL = 2048
HALF = MODEL // 2
PAIRS = 8
PLANE = 16
LINE = 16
ROWS = TOK // PLANE


def split(x):
    high = x.astype(BF16)
    return high, (x - high.astype(F32)).astype(BF16)


def nt(a, b):
    return lax.dot_general(a, b, (((1,), (1,)), ((), ())), preferred_element_type=F32)


def exchange_kernel(
    pair_map, indices, values, target, decoder,
    recon, feat, grad,
    acts_high_t, acts_low_t, dec, dec_high, dec_low, ids_t, vals_t, acts,
    map_send, map_rx, part_send, part_rx, part_own, scale_send, scale_rx, plane_send, plane_rx, layer_sum,
    line_wide,
    line_send, line_rx, err_send, err_rx, err_wide, err_layers, err_pick, err,
    back, picked, pick_rx, pick_wide, pick_line, feat_rx,
    dec_sem, map_ssem, map_rsem, part_ssem, part_rsem, scale_ssem, scale_rsem, plane_ssem, plane_rsem,
    line_ssem, line_rsem, err_ssem, err_rsem, spread_ssem, spread_rsem,
    relay_ssem, relay_rsem, pick_ssem, pick_rsem, feat_ssem, feat_rsem,
):
    p = lax.axis_index("pair")
    f = lax.axis_index("feat")
    y = f // 16
    w = lax.rem(f, 16)
    core = lax.rem(f, 2)
    q = p * 2 + y

    def plane_peer(i):
        same, a, b = i // 8, lax.rem(i, 8) // 2, lax.rem(i, 2)
        far = 2 + jnp.where(a == 1, 3, jnp.where(a == 2, 1, jnp.where(a == 3, 2, 0)))
        x2 = lax.rem(lax.rem(p, 4) + far, 4)
        low2 = lax.rem(p // 4 + 1 - same, 2)
        y2 = lax.rem(y + 1 - b, 2)
        p2 = low2 * 4 + x2
        return p2 * 2 + y2, (p2, y2 * 16 + w)

    def line_peer(i):
        a, b = i // 2, lax.rem(i, 2)
        far = 4 + jnp.where(lax.rem(a, 2) == 1, 8 - (a + 1) // 2, a // 2)
        w2 = lax.rem(w // 2 + far, 8) * 2 + lax.rem(core + 1 - b, 2)
        return w2, (p, y * 16 + w2)

    partner = (p, f + 1 - 2 * core)

    for block in range(4):
        cols = pl.ds(block * 512, 512)
        pltpu.make_async_copy(
            decoder.at[0, :, cols], dec.at[:, cols], dec_sem.at[block]
        ).start()

    barrier = pltpu.get_barrier_semaphore()

    @pl.loop(0, 15)
    def _(d):
        pl.semaphore_signal(barrier, inc=1, device_id=plane_peer(d)[1], device_id_type=MESH)
        pl.semaphore_signal(barrier, inc=1, device_id=line_peer(d)[1], device_id_type=MESH)

    source = pair_map[0, 0]
    goal = pair_map[0, 1]
    row = lax.broadcasted_iota(jnp.int32, (8, 128), 0)
    tile = jnp.where(row < 4, source, goal)
    map_send[...] = tile
    map_rx[p] = tile

    def map_copy(d):
        p2 = lax.rem(p + d, PAIRS)
        return pltpu.make_async_remote_copy(
            src_ref=map_send, dst_ref=map_rx.at[p], send_sem=map_ssem.at[p2],
            recv_sem=map_rsem.at[p], device_id=(p2, f), device_id_type=MESH)

    def map_arrival(d):
        p2 = lax.rem(p + d, PAIRS)
        return pltpu.make_async_remote_copy(
            src_ref=map_send, dst_ref=map_rx.at[p2], send_sem=map_ssem.at[p],
            recv_sem=map_rsem.at[p2], device_id=(p2, f), device_id_type=MESH)

    layer = jnp.minimum(source, LAYERS - 1)
    local = indices[layer] - f * WIDTH
    for k in range(2):
        ids_t[k] = local[k * 128:k * 128 + 128].T
        vals_t[k] = values[layer, k * 128:k * 128 + 128, :].T

    def rows_of(q2):
        return pl.ds(pl.multiple_of(q2 * ROWS, ROWS), ROWS)

    def scale_copy(d):
        q2, peer = plane_peer(d)
        return pltpu.make_async_remote_copy(
            src_ref=scale_send.at[q2], dst_ref=scale_rx.at[q], send_sem=scale_ssem.at[q2],
            recv_sem=scale_rsem.at[q], device_id=peer, device_id_type=MESH)

    def scale_arrival(q2):
        return pltpu.make_async_remote_copy(
            src_ref=scale_send.at[q2], dst_ref=scale_rx.at[q2], send_sem=scale_ssem.at[q],
            recv_sem=scale_rsem.at[q2], device_id=partner, device_id_type=MESH)

    def plane_copy(d):
        q2, peer = plane_peer(d)
        return pltpu.make_async_remote_copy(
            src_ref=plane_send.at[q2], dst_ref=plane_rx.at[q], send_sem=plane_ssem.at[q2],
            recv_sem=plane_rsem.at[q], device_id=peer, device_id_type=MESH)

    def plane_arrival(q2):
        return pltpu.make_async_remote_copy(
            src_ref=plane_send.at[q2], dst_ref=plane_rx.at[q2], send_sem=plane_ssem.at[q],
            recv_sem=plane_rsem.at[q2], device_id=partner, device_id_type=MESH)

    def encode(q2):
        rows = rows_of(q2)
        parts = []
        for m in range(8):
            cols = slice(m * 128, m * 128 + 128)
            parts.append(part_own[rows, cols] + part_rx[rows, cols])
        peak = jnp.abs(parts[0])
        for x in parts[1:]:
            peak = jnp.maximum(peak, jnp.abs(x))
        peak = jnp.maximum(jnp.max(peak, axis=0, keepdims=True), 1e-30)
        inverse = 32000.0 / peak
        codes = [jnp.round(x * inverse).astype(jnp.int16) for x in parts]
        return codes, peak * (1.0 / 32000.0)

    def partial(cols):
        both = jnp.dot(acts[...], dec_high[:, cols], preferred_element_type=F32)
        rest = jnp.dot(acts[0:TOK // 2, :], dec_low[:, cols], preferred_element_type=F32)
        return both[0:TOK // 2] + both[TOK // 2:] + rest

    def tokens_of(same):
        low2 = p // 4 + (1 - 2 * (p // 4)) * (1 - same)
        return low2, pl.ds(pl.multiple_of(low2 * 128, 128), 128)

    def part_copy(same):
        tokens = tokens_of(same)[1]
        return pltpu.make_async_remote_copy(
            src_ref=part_send.at[tokens], dst_ref=part_rx.at[tokens],
            send_sem=part_ssem.at[same], recv_sem=part_rsem.at[same],
            device_id=partner, device_id_type=MESH)

    for same in range(2):
        low2, tokens = tokens_of(same)

        @pl.loop(0, WIDTH // 128)
        def _(block):
            base = pl.multiple_of(block * 128, 128)
            features = lax.broadcasted_iota(jnp.int32, (128, 128), 0) + base

            def step(k, total):
                for j in range(4):
                    ids = ids_t[low2, pl.ds(k * 4 + j, 1), :]
                    vals = vals_t[low2, pl.ds(k * 4 + j, 1), :]
                    total = jnp.where(ids == features, vals, total)
                return total

            total = lax.fori_loop(0, ACTIVE // 4, step, jnp.zeros((128, 128), F32))
            high, low = split(total)
            acts_high_t[pl.ds(base, 128), tokens] = high
            acts_low_t[pl.ds(base, 128), tokens] = low
            high, low = split(total.T)
            cols = pl.ds(pl.multiple_of(base, 128), 128)
            acts[0:TOK // 2, cols] = high
            acts[TOK // 2:, cols] = low

        if same == 0:
            for block in range(4):
                cols = pl.ds(block * 512, 512)
                pltpu.make_async_copy(
                    decoder.at[0, :, cols], dec.at[:, cols], dec_sem.at[block]
                ).wait()

            @pl.loop(0, WIDTH // 16)
            def _(block):
                rows = pl.ds(block * 16, 16)
                high, low = split(dec[rows, :])
                dec_high[rows, :] = high
                dec_low[rows, :] = low

        part_send[tokens, :] = partial(pl.ds(pl.multiple_of((1 - core) * HALF, HALF), HALF))

        if same == 0:
            pl.semaphore_wait(barrier, 30)

        part_copy(same).start()

        if same == 0:
            @pl.loop(1, PAIRS)
            def _(d):
                map_copy(d).start()

        part_own[tokens, :] = partial(pl.ds(pl.multiple_of(core * HALF, HALF), HALF))
        part_copy(same).wait_recv()

        @pl.loop(8 * same, 8 + 7 * same)
        def _(d):
            q2 = plane_peer(d)[0]
            codes, scale = encode(q2)
            scale_send[q2] = scale
            for m in range(8):
                plane_send[q2, :, m * 128:m * 128 + 128] = codes[m]
            scale_copy(d).start()
            plane_copy(d).start()

    codes, scale = encode(q)
    scale_rx[q] = scale
    for m in range(8):
        plane_rx[q, :, m * 128:m * 128 + 128] = codes[m]

    @pl.loop(1, PAIRS)
    def _(d):
        map_arrival(d).wait_recv()

    layer_sum[...] = jnp.zeros_like(layer_sum)

    def add_pair(q2, q3):
        scales = [jnp.concatenate([scale_rx[k]] * 8, axis=1) for k in (q2, q3)]
        both = plane_rx[q2].astype(F32) * scales[0] + plane_rx[q3].astype(F32) * scales[1]
        goal2 = map_rx[q2 // 2, 4:5, 0:1]
        for l in range(LAYERS):
            layer_sum[l] += jnp.where(goal2 == l, both, 0.0)

    def wait_plane(q2):
        plane_arrival(q2).wait_recv()
        scale_arrival(q2).wait_recv()

    @pl.loop(0, 7)
    def _(j):
        q2, q3 = plane_peer(2 * j)[0], plane_peer(2 * j + 1)[0]
        wait_plane(q2)
        wait_plane(q3)
        add_pair(q2, q3)

    q2 = plane_peer(14)[0]
    wait_plane(q2)
    add_pair(q2, q)

    tiles = [(l, m, layer_sum[l, :, m * 128:m * 128 + 128]) for l in range(LAYERS) for m in range(8)]
    peak = jnp.full((ROWS, 128), 1e-30, F32)
    for _, _, x in tiles:
        peak = jnp.maximum(peak, jnp.abs(x))
    power = jnp.ceil(jnp.log2(peak * (1.0 / 32000.0)))
    inverse = jnp.exp2(-power)
    for l, m, x in tiles:
        line_wide[pl.ds(l * 8 + m, 16, stride=32), :] = jnp.round(x * inverse)
    for m in range(8):
        line_wide[pl.ds(24 + m, 16, stride=32), :] = power
    for w2 in range(LINE):
        line_send[w2] = line_wide[w2 * 32:w2 * 32 + 32, :].astype(jnp.int16)

    def line_copy(d):
        w2, peer = line_peer(d)
        return pltpu.make_async_remote_copy(
            src_ref=line_send.at[w2], dst_ref=line_rx.at[w], send_sem=line_ssem.at[w2],
            recv_sem=line_rsem.at[w], device_id=peer, device_id_type=MESH)

    def line_arrival(w2):
        return pltpu.make_async_remote_copy(
            src_ref=line_send.at[w2], dst_ref=line_rx.at[w2], send_sem=line_ssem.at[w],
            recv_sem=line_rsem.at[w2], device_id=partner, device_id_type=MESH)

    @pl.loop(0, 15)
    def _(d):
        line_copy(d).start()

    line_rx[w] = line_send[w]

    @pl.loop(0, 15)
    def _(d):
        line_arrival(line_peer(d)[0]).wait_recv()

    for half in range(2):
        total = jnp.zeros((24, 128), F32)
        for z2 in range(8):
            piece = line_rx[2 * z2 + half].astype(F32)
            total = total + piece[0:24] * jnp.exp2(piece[24:25])
        for l in range(LAYERS):
            part = total[l * 8:l * 8 + 8]
            rows = slice(half * 8, half * 8 + 8)
            recon[l, rows, :] = part
            err_send[half, l * 8:l * 8 + 8, :] = (part - target[l, rows, :]).astype(BF16)

    def err_copy(d):
        w2, peer = line_peer(d)
        return pltpu.make_async_remote_copy(
            src_ref=err_send.at[lax.rem(w2, 2)], dst_ref=err_rx.at[w], send_sem=err_ssem.at[w2],
            recv_sem=err_rsem.at[w], device_id=peer, device_id_type=MESH)

    def err_arrival(w2):
        return pltpu.make_async_remote_copy(
            src_ref=err_send.at[0], dst_ref=err_rx.at[w2], send_sem=err_ssem.at[w],
            recv_sem=err_rsem.at[w2], device_id=partner, device_id_type=MESH)

    @pl.loop(0, 15)
    def _(d):
        err_copy(d).start()

    err_rx[w] = err_send[core]

    @pl.loop(0, 15)
    def _(d):
        err_arrival(line_peer(d)[0]).wait_recv()

    @pl.loop(0, LINE)
    def _(w2):
        err_wide[pl.ds(pl.multiple_of(w2 * 24, 8), 24), :] = err_rx[w2].astype(F32)

    for l in range(LAYERS):
        for m in range(8):
            err_layers[l, :, m * 128:m * 128 + 128] = err_wide[pl.ds(l * 8 + m, 16, stride=24), :]

    def spread_copy(d):
        q2, peer = plane_peer(d)
        return pltpu.make_async_remote_copy(
            src_ref=err_pick.at[q2 // 2], dst_ref=err.at[core, rows_of(q)], send_sem=spread_ssem.at[q2],
            recv_sem=spread_rsem.at[q], device_id=peer, device_id_type=MESH)

    def spread_arrival(q2):
        return pltpu.make_async_remote_copy(
            src_ref=err_pick.at[0], dst_ref=err.at[core, rows_of(q2)], send_sem=spread_ssem.at[q],
            recv_sem=spread_rsem.at[q2], device_id=partner, device_id_type=MESH)

    def relay_copy(q2):
        piece = err.at[core, rows_of(q2)]
        return pltpu.make_async_remote_copy(
            src_ref=piece, dst_ref=piece, send_sem=relay_ssem.at[q2],
            recv_sem=relay_rsem.at[q2], device_id=partner, device_id_type=MESH)

    def relay_arrival(q2):
        piece = err.at[1 - core, rows_of(q2)]
        return pltpu.make_async_remote_copy(
            src_ref=piece, dst_ref=piece, send_sem=relay_ssem.at[q2],
            recv_sem=relay_rsem.at[q2], device_id=partner, device_id_type=MESH)

    def choose(p2):
        goal2 = map_rx[p2, 4:5, 0:1]
        chosen = jnp.zeros((ROWS, HALF), F32)
        for l in range(LAYERS):
            chosen = jnp.where(goal2 == l, err_layers[l], chosen)
        err_pick[p2] = chosen.astype(BF16)

    @pl.loop(0, 7)
    def _(j):
        choose(plane_peer(2 * j)[0] // 2)
        spread_copy(2 * j).start()
        spread_copy(2 * j + 1).start()

    choose(p)
    spread_copy(14).start()
    err[core, rows_of(q), :] = err_pick[p]
    relay_copy(q).start()

    def pick_copy(d):
        q2, peer = plane_peer(d)
        return pltpu.make_async_remote_copy(
            src_ref=picked.at[rows_of(q2)], dst_ref=pick_rx.at[q], send_sem=pick_ssem.at[q2],
            recv_sem=pick_rsem.at[q], device_id=peer, device_id_type=MESH)

    def pick_arrival(q2):
        return pltpu.make_async_remote_copy(
            src_ref=picked.at[rows_of(q2)], dst_ref=pick_rx.at[q2], send_sem=pick_ssem.at[q],
            recv_sem=pick_rsem.at[q2], device_id=partner, device_id_type=MESH)

    def back_of(half):
        cols = pl.ds(pl.multiple_of(half * HALF, HALF), HALF)
        e = err[half]
        return nt(e, dec_high[:, cols]) + nt(e, dec_low[:, cols])

    @pl.loop(0, 15)
    def _(d):
        q2 = plane_peer(d)[0]
        spread_arrival(q2).wait_recv()
        relay_copy(q2).start()

    back[...] = back_of(core)

    @pl.loop(0, PLANE)
    def _(q2):
        relay_arrival(q2).wait_recv()

    back[...] += back_of(1 - core)
    local = indices[layer] - f * WIDTH
    lane = jnp.bitwise_and(local, 127)
    block_of = jnp.right_shift(local, 7)
    found = jnp.zeros((TOK, ACTIVE), F32)
    for n in range(WIDTH // 128):
        here = jnp.take_along_axis(back[:, n * 128:n * 128 + 128], lane, axis=1)
        found = jnp.where(block_of == n, here, found)
    picked[...] = found

    @pl.loop(0, 15)
    def _(d):
        pick_copy(d).start()

    for half in range(2):
        cols = slice(half * HALF, half * HALF + HALF)
        e = err[half]
        grad[:, cols] = jnp.dot(acts_high_t[...], e, preferred_element_type=F32) + jnp.dot(
            acts_low_t[...], e, preferred_element_type=F32)

    pick_rx[q] = picked[rows_of(q), :]
    pick_wide[...] = jnp.zeros_like(pick_wide)

    @pl.loop(0, 15)
    def _(d):
        pick_arrival(plane_peer(d)[0]).wait_recv()

    sums = [jnp.zeros((ROWS, ACTIVE), F32) for _ in range(LAYERS)]
    for p2 in range(PAIRS):
        both = pick_rx[2 * p2] + pick_rx[2 * p2 + 1]
        source2 = map_rx[p2, 0:1, 0:1]
        for l in range(LAYERS):
            sums[l] = sums[l] + jnp.where(source2 == l, both, 0.0)
    for l in range(LAYERS):
        pick_wide[pl.ds(l, 16, stride=8), :] = sums[l]

    for w2 in range(LINE):
        pick_line[w2] = pick_wide[w2 * 8:w2 * 8 + 4, :]

    def feat_copy(d):
        w2, peer = line_peer(d)
        return pltpu.make_async_remote_copy(
            src_ref=pick_line.at[w2], dst_ref=feat_rx.at[w],
            send_sem=feat_ssem.at[w2], recv_sem=feat_rsem.at[w], device_id=peer, device_id_type=MESH)

    def feat_arrival(w2):
        return pltpu.make_async_remote_copy(
            src_ref=pick_line.at[w2], dst_ref=feat_rx.at[w2],
            send_sem=feat_ssem.at[w], recv_sem=feat_rsem.at[w2], device_id=partner, device_id_type=MESH)

    @pl.loop(0, 15)
    def _(d):
        feat_copy(d).start()

    feat_rx[w] = pick_line[w]

    @pl.loop(0, 15)
    def _(d):
        feat_arrival(line_peer(d)[0]).wait_recv()

    total = feat_rx[0]
    for w2 in range(1, LINE):
        total = total + feat_rx[w2]
    feat[...] = total[0:LAYERS]

    @pl.loop(1, PAIRS)
    def _(d):
        map_copy(d).wait_send()

    @pl.loop(0, 15)
    def _(d):
        scale_copy(d).wait_send()
        plane_copy(d).wait_send()
        line_copy(d).wait_send()
        err_copy(d).wait_send()
        spread_copy(d).wait_send()
        pick_copy(d).wait_send()
        feat_copy(d).wait_send()

    for same in range(2):
        part_copy(same).wait_send()

    @pl.loop(0, PLANE)
    def _(q2):
        relay_copy(q2).wait_send()


def output_kernel(grad, recon, feat, out, recon_out, feat_out, sem):
    copies = [
        pltpu.make_async_copy(
            grad.at[pl.ds(k * 128, 128)], out.at[pl.ds(k * 128, 128)], sem.at[k])
        for k in range(WIDTH // 128)
    ]
    for copy in copies:
        copy.start()
    for k in range(16):
        recon_out[:, k * 128:k * 128 + 128] = recon[:, k, :].astype(BF16)
    for l in range(LAYERS):
        feat_out[l] = feat[l:l + 1, :]
    for copy in copies:
        copy.wait()


def body(decoder, pair_map, indices, values, target):
    vmem = pl.BlockSpec(memory_space=pltpu.VMEM)
    dma = pltpu.SemaphoreType.DMA
    recon, feat, grad = pl.pallas_call(
        exchange_kernel,
        out_shape=(
            pltpu.VMEM((LAYERS, 16, 128), F32),
            pltpu.VMEM((LAYERS, ACTIVE), F32),
            pltpu.VMEM((WIDTH, MODEL), F32),
        ),
        in_specs=[pl.BlockSpec(memory_space=pltpu.SMEM), vmem, vmem, vmem, pl.BlockSpec(memory_space=pl.ANY)],
        out_specs=(vmem, vmem, vmem),
        scratch_shapes=[
            pltpu.VMEM((WIDTH, TOK), BF16),
            pltpu.VMEM((WIDTH, TOK), BF16),
            pltpu.VMEM((WIDTH, MODEL), F32),
            pltpu.VMEM((WIDTH, MODEL), BF16),
            pltpu.VMEM((WIDTH, MODEL), BF16),
            pltpu.VMEM((2, ACTIVE, TOK // 2), jnp.int32),
            pltpu.VMEM((2, ACTIVE, TOK // 2), F32),
            pltpu.VMEM((TOK, WIDTH), BF16),
            pltpu.VMEM((8, 128), jnp.int32),
            pltpu.VMEM((PAIRS, 8, 128), jnp.int32),
            pltpu.VMEM((TOK, HALF), F32),
            pltpu.VMEM((TOK, HALF), F32),
            pltpu.VMEM((TOK, HALF), F32),
            pltpu.VMEM((PLANE, 1, 128), F32),
            pltpu.VMEM((PLANE, 1, 128), F32),
            pltpu.VMEM((PLANE, ROWS, HALF), jnp.int16),
            pltpu.VMEM((PLANE, ROWS, HALF), jnp.int16),
            pltpu.VMEM((LAYERS, ROWS, HALF), F32),
            pltpu.VMEM((LINE * 32, 128), F32),
            pltpu.VMEM((LINE, 32, 128), jnp.int16),
            pltpu.VMEM((LINE, 32, 128), jnp.int16),
            pltpu.VMEM((2, 24, 128), BF16),
            pltpu.VMEM((LINE, 24, 128), BF16),
            pltpu.VMEM((LINE * 24, 128), F32),
            pltpu.VMEM((LAYERS, ROWS, HALF), F32),
            pltpu.VMEM((PAIRS, ROWS, HALF), BF16),
            pltpu.VMEM((2, TOK, HALF), BF16),
            pltpu.VMEM((TOK, WIDTH), F32),
            pltpu.VMEM((TOK, ACTIVE), F32),
            pltpu.VMEM((PLANE, ROWS, ACTIVE), F32),
            pltpu.VMEM((LINE * 8, 128), F32),
            pltpu.VMEM((LINE, 4, 128), F32),
            pltpu.VMEM((LINE, 4, 128), F32),
            dma((4,)),
            dma((PAIRS,)), dma((PAIRS,)),
            dma((2,)), dma((2,)),
            dma((PLANE,)), dma((PLANE,)),
            dma((PLANE,)), dma((PLANE,)),
            dma((LINE,)), dma((LINE,)),
            dma((LINE,)), dma((LINE,)),
            dma((PLANE,)), dma((PLANE,)),
            dma((PLANE,)), dma((PLANE,)),
            dma((PLANE,)), dma((PLANE,)),
            dma((LINE,)), dma((LINE,)),
        ],
        compiler_params=pltpu.CompilerParams(
            collective_id=0, has_side_effects=True, vmem_limit_bytes=59 * 2**20
        ),
    )(pair_map, indices, values, target.reshape(LAYERS, 16, 128), decoder)
    dec_grad, recon, feat = pl.pallas_call(
        output_kernel,
        out_shape=(
            jax.ShapeDtypeStruct((WIDTH, MODEL), F32),
            jax.ShapeDtypeStruct((LAYERS, MODEL), BF16),
            jax.ShapeDtypeStruct((LAYERS, 1, ACTIVE), F32),
        ),
        in_specs=[vmem, vmem, vmem],
        out_specs=(pl.BlockSpec(memory_space=pl.ANY), vmem, vmem),
        scratch_shapes=[dma((WIDTH // 128,))],
        compiler_params=pltpu.CompilerParams(vmem_limit_bytes=59 * 2**20),
    )(*(pltpu.with_memory_space_constraint(x, pltpu.VMEM) for x in (grad, recon, feat)))
    return recon.reshape(LAYERS, 1, MODEL), dec_grad.reshape(1, WIDTH, MODEL), feat


def solution(mesh):
    in_specs = (P("pair", "feat", None), P("pair", None), P(), P(), P(None, ("pair", "feat"), None))
    out_specs = (
        P(None, ("pair", "feat"), None),
        P("pair", "feat", None),
        P(None, ("pair", "feat"), None),
    )
    return jax.shard_map(body, mesh=mesh, in_specs=in_specs, out_specs=out_specs, check_vma=False)
```

```python
import jax
import jax.numpy as jnp
from jax import lax
from jax.experimental import pallas as pl
from jax.experimental.pallas import tpu as pltpu
from jax.sharding import PartitionSpec as P

MESH = pl.DeviceIdType.MESH
F32 = jnp.float32
BF16 = jnp.bfloat16

LAYERS = 3
TOK = 256
ACTIVE = 128
WIDTH = 512
MODEL = 2048
HALF = MODEL // 2
PAIRS = 8
PLANE = 16
LINE = 16
ROWS = TOK // PLANE


def split(x):
    high = x.astype(BF16)
    return high, (x - high.astype(F32)).astype(BF16)


def nt(a, b):
    return lax.dot_general(a, b, (((1,), (1,)), ((), ())), preferred_element_type=F32)


def exchange_kernel(
    pair_map, indices, values, target, decoder,
    recon, feat, grad,
    acts_high_t, acts_low_t, dec, dec_high, dec_low, ids_t, vals_t, acts,
    map_send, map_rx, part_send, part_rx, part_own, scale_send, scale_rx, plane_send, plane_rx, layer_sum,
    line_wide,
    line_send, line_rx, err_send, err_rx, err_wide, err_layers, err_pick, err,
    back, picked, pick_rx, pick_wide, pick_line, feat_rx,
    dec_sem, map_ssem, map_rsem, part_ssem, part_rsem, scale_ssem, scale_rsem, plane_ssem, plane_rsem,
    line_ssem, line_rsem, err_ssem, err_rsem, spread_ssem, spread_rsem,
    relay_ssem, relay_rsem, pick_ssem, pick_rsem, feat_ssem, feat_rsem,
):
    p = lax.axis_index("pair")
    f = lax.axis_index("feat")
    y = f // 16
    w = lax.rem(f, 16)
    core = lax.rem(f, 2)
    q = p * 2 + y

    def plane_peer(i):
        same, a, b = i // 8, lax.rem(i, 8) // 2, lax.rem(i, 2)
        far = 2 + jnp.where(a == 1, 3, jnp.where(a == 2, 1, jnp.where(a == 3, 2, 0)))
        x2 = lax.rem(lax.rem(p, 4) + far, 4)
        low2 = lax.rem(p // 4 + 1 - same, 2)
        y2 = lax.rem(y + 1 - b, 2)
        p2 = low2 * 4 + x2
        return p2 * 2 + y2, (p2, y2 * 16 + w)

    def line_peer(i):
        a, b = i // 2, lax.rem(i, 2)
        far = 4 + jnp.where(lax.rem(a, 2) == 1, 8 - (a + 1) // 2, a // 2)
        w2 = lax.rem(w // 2 + far, 8) * 2 + lax.rem(core + 1 - b, 2)
        return w2, (p, y * 16 + w2)

    partner = (p, f + 1 - 2 * core)

    for block in range(4):
        cols = pl.ds(block * 512, 512)
        pltpu.make_async_copy(
            decoder.at[0, :, cols], dec.at[:, cols], dec_sem.at[block]
        ).start()

    barrier = pltpu.get_barrier_semaphore()

    @pl.loop(0, 15)
    def _(d):
        pl.semaphore_signal(barrier, inc=1, device_id=plane_peer(d)[1], device_id_type=MESH)
        pl.semaphore_signal(barrier, inc=1, device_id=line_peer(d)[1], device_id_type=MESH)

    source = pair_map[0, 0]
    goal = pair_map[0, 1]
    row = lax.broadcasted_iota(jnp.int32, (8, 128), 0)
    tile = jnp.where(row < 4, source, goal)
    map_send[...] = tile
    map_rx[p] = tile

    def map_copy(d):
        p2 = lax.rem(p + d, PAIRS)
        return pltpu.make_async_remote_copy(
            src_ref=map_send, dst_ref=map_rx.at[p], send_sem=map_ssem.at[p2],
            recv_sem=map_rsem.at[p], device_id=(p2, f), device_id_type=MESH)

    def map_arrival(d):
        p2 = lax.rem(p + d, PAIRS)
        return pltpu.make_async_remote_copy(
            src_ref=map_send, dst_ref=map_rx.at[p2], send_sem=map_ssem.at[p],
            recv_sem=map_rsem.at[p2], device_id=(p2, f), device_id_type=MESH)

    layer = jnp.minimum(source, LAYERS - 1)
    local = indices[layer] - f * WIDTH
    for k in range(2):
        ids_t[k] = local[k * 128:k * 128 + 128].T
        vals_t[k] = values[layer, k * 128:k * 128 + 128, :].T

    def rows_of(q2):
        return pl.ds(pl.multiple_of(q2 * ROWS, ROWS), ROWS)

    def scale_copy(d):
        q2, peer = plane_peer(d)
        return pltpu.make_async_remote_copy(
            src_ref=scale_send.at[q2], dst_ref=scale_rx.at[q], send_sem=scale_ssem.at[q2],
            recv_sem=scale_rsem.at[q], device_id=peer, device_id_type=MESH)

    def scale_arrival(q2):
        return pltpu.make_async_remote_copy(
            src_ref=scale_send.at[q2], dst_ref=scale_rx.at[q2], send_sem=scale_ssem.at[q],
            recv_sem=scale_rsem.at[q2], device_id=partner, device_id_type=MESH)

    def plane_copy(d):
        q2, peer = plane_peer(d)
        return pltpu.make_async_remote_copy(
            src_ref=plane_send.at[q2], dst_ref=plane_rx.at[q], send_sem=plane_ssem.at[q2],
            recv_sem=plane_rsem.at[q], device_id=peer, device_id_type=MESH)

    def plane_arrival(q2):
        return pltpu.make_async_remote_copy(
            src_ref=plane_send.at[q2], dst_ref=plane_rx.at[q2], send_sem=plane_ssem.at[q],
            recv_sem=plane_rsem.at[q2], device_id=partner, device_id_type=MESH)

    def encode(q2):
        rows = rows_of(q2)
        parts = []
        for m in range(8):
            cols = slice(m * 128, m * 128 + 128)
            parts.append(part_own[rows, cols] + part_rx[rows, cols])
        peak = jnp.abs(parts[0])
        for x in parts[1:]:
            peak = jnp.maximum(peak, jnp.abs(x))
        peak = jnp.maximum(jnp.max(peak, axis=0, keepdims=True), 1e-30)
        inverse = 32000.0 / peak
        codes = [jnp.round(x * inverse).astype(jnp.int16) for x in parts]
        return codes, peak * (1.0 / 32000.0)

    def partial(cols):
        both = jnp.dot(acts[...], dec_high[:, cols], preferred_element_type=F32)
        rest = jnp.dot(acts[0:TOK // 2, :], dec_low[:, cols], preferred_element_type=F32)
        return both[0:TOK // 2] + both[TOK // 2:] + rest

    def tokens_of(same):
        low2 = p // 4 + (1 - 2 * (p // 4)) * (1 - same)
        return low2, pl.ds(pl.multiple_of(low2 * 128, 128), 128)

    def part_copy(same):
        tokens = tokens_of(same)[1]
        return pltpu.make_async_remote_copy(
            src_ref=part_send.at[tokens], dst_ref=part_rx.at[tokens],
            send_sem=part_ssem.at[same], recv_sem=part_rsem.at[same],
            device_id=partner, device_id_type=MESH)

    for same in range(2):
        low2, tokens = tokens_of(same)

        @pl.loop(0, WIDTH // 128)
        def _(block):
            base = pl.multiple_of(block * 128, 128)
            features = lax.broadcasted_iota(jnp.int32, (128, 128), 0) + base

            def step(k, total):
                for j in range(16):
                    ids = ids_t[low2, pl.ds(k * 16 + j, 1), :]
                    vals = vals_t[low2, pl.ds(k * 16 + j, 1), :]
                    total = jnp.where(ids == features, vals, total)
                return total

            total = lax.fori_loop(0, ACTIVE // 16, step, jnp.zeros((128, 128), F32))
            high, low = split(total)
            acts_high_t[pl.ds(base, 128), tokens] = high
            acts_low_t[pl.ds(base, 128), tokens] = low
            high, low = split(total.T)
            cols = pl.ds(pl.multiple_of(base, 128), 128)
            acts[0:TOK // 2, cols] = high
            acts[TOK // 2:, cols] = low

        if same == 0:
            for block in range(4):
                cols = pl.ds(block * 512, 512)
                pltpu.make_async_copy(
                    decoder.at[0, :, cols], dec.at[:, cols], dec_sem.at[block]
                ).wait()

            @pl.loop(0, WIDTH // 16)
            def _(block):
                rows = pl.ds(block * 16, 16)
                high, low = split(dec[rows, :])
                dec_high[rows, :] = high
                dec_low[rows, :] = low

        part_send[tokens, :] = partial(pl.ds(pl.multiple_of((1 - core) * HALF, HALF), HALF))

        if same == 0:
            pl.semaphore_wait(barrier, 30)

        part_copy(same).start()

        if same == 0:
            @pl.loop(1, PAIRS)
            def _(d):
                map_copy(d).start()

        part_own[tokens, :] = partial(pl.ds(pl.multiple_of(core * HALF, HALF), HALF))
        part_copy(same).wait_recv()

        @pl.loop(8 * same, 8 + 7 * same)
        def _(d):
            q2 = plane_peer(d)[0]
            codes, scale = encode(q2)
            scale_send[q2] = scale
            for m in range(8):
                plane_send[q2, :, m * 128:m * 128 + 128] = codes[m]
            scale_copy(d).start()
            plane_copy(d).start()

    codes, scale = encode(q)
    scale_rx[q] = scale
    for m in range(8):
        plane_rx[q, :, m * 128:m * 128 + 128] = codes[m]

    @pl.loop(1, PAIRS)
    def _(d):
        map_arrival(d).wait_recv()

    layer_sum[...] = jnp.zeros_like(layer_sum)

    def add_pair(q2, q3):
        scales = [jnp.concatenate([scale_rx[k]] * 8, axis=1) for k in (q2, q3)]
        both = plane_rx[q2].astype(F32) * scales[0] + plane_rx[q3].astype(F32) * scales[1]
        goal2 = map_rx[q2 // 2, 4:5, 0:1]
        for l in range(LAYERS):
            layer_sum[l] += jnp.where(goal2 == l, both, 0.0)

    def wait_plane(q2):
        plane_arrival(q2).wait_recv()
        scale_arrival(q2).wait_recv()

    @pl.loop(0, 7)
    def _(j):
        q2, q3 = plane_peer(2 * j)[0], plane_peer(2 * j + 1)[0]
        wait_plane(q2)
        wait_plane(q3)
        add_pair(q2, q3)

    q2 = plane_peer(14)[0]
    wait_plane(q2)
    add_pair(q2, q)

    tiles = [(l, m, layer_sum[l, :, m * 128:m * 128 + 128]) for l in range(LAYERS) for m in range(8)]
    peak = jnp.full((ROWS, 128), 1e-30, F32)
    for _, _, x in tiles:
        peak = jnp.maximum(peak, jnp.abs(x))
    power = jnp.ceil(jnp.log2(peak * (1.0 / 32000.0)))
    inverse = jnp.exp2(-power)
    for l, m, x in tiles:
        line_wide[pl.ds(l * 8 + m, 16, stride=32), :] = jnp.round(x * inverse)
    for m in range(8):
        line_wide[pl.ds(24 + m, 16, stride=32), :] = power
    for w2 in range(LINE):
        line_send[w2] = line_wide[w2 * 32:w2 * 32 + 32, :].astype(jnp.int16)

    def line_copy(d):
        w2, peer = line_peer(d)
        return pltpu.make_async_remote_copy(
            src_ref=line_send.at[w2], dst_ref=line_rx.at[w], send_sem=line_ssem.at[w2],
            recv_sem=line_rsem.at[w], device_id=peer, device_id_type=MESH)

    def line_arrival(w2):
        return pltpu.make_async_remote_copy(
            src_ref=line_send.at[w2], dst_ref=line_rx.at[w2], send_sem=line_ssem.at[w],
            recv_sem=line_rsem.at[w2], device_id=partner, device_id_type=MESH)

    @pl.loop(0, 15)
    def _(d):
        line_copy(d).start()

    line_rx[w] = line_send[w]

    @pl.loop(0, 15)
    def _(d):
        line_arrival(line_peer(d)[0]).wait_recv()

    for half in range(2):
        total = jnp.zeros((24, 128), F32)
        for z2 in range(8):
            piece = line_rx[2 * z2 + half].astype(F32)
            total = total + piece[0:24] * jnp.exp2(piece[24:25])
        for l in range(LAYERS):
            part = total[l * 8:l * 8 + 8]
            rows = slice(half * 8, half * 8 + 8)
            recon[l, rows, :] = part
            err_send[half, l * 8:l * 8 + 8, :] = (part - target[l, rows, :]).astype(BF16)

    def err_copy(d):
        w2, peer = line_peer(d)
        return pltpu.make_async_remote_copy(
            src_ref=err_send.at[lax.rem(w2, 2)], dst_ref=err_rx.at[w], send_sem=err_ssem.at[w2],
            recv_sem=err_rsem.at[w], device_id=peer, device_id_type=MESH)

    def err_arrival(w2):
        return pltpu.make_async_remote_copy(
            src_ref=err_send.at[0], dst_ref=err_rx.at[w2], send_sem=err_ssem.at[w],
            recv_sem=err_rsem.at[w2], device_id=partner, device_id_type=MESH)

    @pl.loop(0, 15)
    def _(d):
        err_copy(d).start()

    err_rx[w] = err_send[core]

    @pl.loop(0, 15)
    def _(d):
        err_arrival(line_peer(d)[0]).wait_recv()

    @pl.loop(0, LINE)
    def _(w2):
        err_wide[pl.ds(pl.multiple_of(w2 * 24, 8), 24), :] = err_rx[w2].astype(F32)

    for l in range(LAYERS):
        for m in range(8):
            err_layers[l, :, m * 128:m * 128 + 128] = err_wide[pl.ds(l * 8 + m, 16, stride=24), :]

    def spread_copy(d):
        q2, peer = plane_peer(d)
        return pltpu.make_async_remote_copy(
            src_ref=err_pick.at[q2 // 2], dst_ref=err.at[core, rows_of(q)], send_sem=spread_ssem.at[q2],
            recv_sem=spread_rsem.at[q], device_id=peer, device_id_type=MESH)

    def spread_arrival(q2):
        return pltpu.make_async_remote_copy(
            src_ref=err_pick.at[0], dst_ref=err.at[core, rows_of(q2)], send_sem=spread_ssem.at[q],
            recv_sem=spread_rsem.at[q2], device_id=partner, device_id_type=MESH)

    def relay_copy(q2):
        piece = err.at[core, rows_of(q2)]
        return pltpu.make_async_remote_copy(
            src_ref=piece, dst_ref=piece, send_sem=relay_ssem.at[q2],
            recv_sem=relay_rsem.at[q2], device_id=partner, device_id_type=MESH)

    def relay_arrival(q2):
        piece = err.at[1 - core, rows_of(q2)]
        return pltpu.make_async_remote_copy(
            src_ref=piece, dst_ref=piece, send_sem=relay_ssem.at[q2],
            recv_sem=relay_rsem.at[q2], device_id=partner, device_id_type=MESH)

    def choose(p2):
        goal2 = map_rx[p2, 4:5, 0:1]
        chosen = jnp.zeros((ROWS, HALF), F32)
        for l in range(LAYERS):
            chosen = jnp.where(goal2 == l, err_layers[l], chosen)
        err_pick[p2] = chosen.astype(BF16)

    @pl.loop(0, 7)
    def _(j):
        choose(plane_peer(2 * j)[0] // 2)
        spread_copy(2 * j).start()
        spread_copy(2 * j + 1).start()

    choose(p)
    spread_copy(14).start()
    err[core, rows_of(q), :] = err_pick[p]
    relay_copy(q).start()

    def pick_copy(d):
        q2, peer = plane_peer(d)
        return pltpu.make_async_remote_copy(
            src_ref=picked.at[rows_of(q2)], dst_ref=pick_rx.at[q], send_sem=pick_ssem.at[q2],
            recv_sem=pick_rsem.at[q], device_id=peer, device_id_type=MESH)

    def pick_arrival(q2):
        return pltpu.make_async_remote_copy(
            src_ref=picked.at[rows_of(q2)], dst_ref=pick_rx.at[q2], send_sem=pick_ssem.at[q],
            recv_sem=pick_rsem.at[q2], device_id=partner, device_id_type=MESH)

    def back_of(half):
        cols = pl.ds(pl.multiple_of(half * HALF, HALF), HALF)
        e = err[half]
        return nt(e, dec_high[:, cols]) + nt(e, dec_low[:, cols])

    @pl.loop(0, 15)
    def _(d):
        q2 = plane_peer(d)[0]
        spread_arrival(q2).wait_recv()
        relay_copy(q2).start()

    back[...] = back_of(core)

    @pl.loop(0, PLANE)
    def _(q2):
        relay_arrival(q2).wait_recv()

    back[...] += back_of(1 - core)
    local = indices[layer] - f * WIDTH
    lane = jnp.bitwise_and(local, 127)
    block_of = jnp.right_shift(local, 7)
    found = jnp.zeros((TOK, ACTIVE), F32)
    for n in range(WIDTH // 128):
        here = jnp.take_along_axis(back[:, n * 128:n * 128 + 128], lane, axis=1)
        found = jnp.where(block_of == n, here, found)
    picked[...] = found

    @pl.loop(0, 15)
    def _(d):
        pick_copy(d).start()

    for half in range(2):
        cols = slice(half * HALF, half * HALF + HALF)
        e = err[half]
        grad[:, cols] = jnp.dot(acts_high_t[...], e, preferred_element_type=F32) + jnp.dot(
            acts_low_t[...], e, preferred_element_type=F32)

    pick_rx[q] = picked[rows_of(q), :]
    pick_wide[...] = jnp.zeros_like(pick_wide)

    @pl.loop(0, 15)
    def _(d):
        pick_arrival(plane_peer(d)[0]).wait_recv()

    sums = [jnp.zeros((ROWS, ACTIVE), F32) for _ in range(LAYERS)]
    for p2 in range(PAIRS):
        both = pick_rx[2 * p2] + pick_rx[2 * p2 + 1]
        source2 = map_rx[p2, 0:1, 0:1]
        for l in range(LAYERS):
            sums[l] = sums[l] + jnp.where(source2 == l, both, 0.0)
    for l in range(LAYERS):
        pick_wide[pl.ds(l, 16, stride=8), :] = sums[l]

    for w2 in range(LINE):
        pick_line[w2] = pick_wide[w2 * 8:w2 * 8 + 4, :]

    def feat_copy(d):
        w2, peer = line_peer(d)
        return pltpu.make_async_remote_copy(
            src_ref=pick_line.at[w2], dst_ref=feat_rx.at[w],
            send_sem=feat_ssem.at[w2], recv_sem=feat_rsem.at[w], device_id=peer, device_id_type=MESH)

    def feat_arrival(w2):
        return pltpu.make_async_remote_copy(
            src_ref=pick_line.at[w2], dst_ref=feat_rx.at[w2],
            send_sem=feat_ssem.at[w], recv_sem=feat_rsem.at[w2], device_id=partner, device_id_type=MESH)

    @pl.loop(0, 15)
    def _(d):
        feat_copy(d).start()

    feat_rx[w] = pick_line[w]

    @pl.loop(0, 15)
    def _(d):
        feat_arrival(line_peer(d)[0]).wait_recv()

    total = feat_rx[0]
    for w2 in range(1, LINE):
        total = total + feat_rx[w2]
    feat[...] = total[0:LAYERS]

    @pl.loop(1, PAIRS)
    def _(d):
        map_copy(d).wait_send()

    @pl.loop(0, 15)
    def _(d):
        scale_copy(d).wait_send()
        plane_copy(d).wait_send()
        line_copy(d).wait_send()
        err_copy(d).wait_send()
        spread_copy(d).wait_send()
        pick_copy(d).wait_send()
        feat_copy(d).wait_send()

    for same in range(2):
        part_copy(same).wait_send()

    @pl.loop(0, PLANE)
    def _(q2):
        relay_copy(q2).wait_send()


def output_kernel(grad, recon, feat, out, recon_out, feat_out, sem):
    copies = [
        pltpu.make_async_copy(
            grad.at[pl.ds(k * 128, 128)], out.at[pl.ds(k * 128, 128)], sem.at[k])
        for k in range(WIDTH // 128)
    ]
    for copy in copies:
        copy.start()
    for k in range(16):
        recon_out[:, k * 128:k * 128 + 128] = recon[:, k, :].astype(BF16)
    for l in range(LAYERS):
        feat_out[l] = feat[l:l + 1, :]
    for copy in copies:
        copy.wait()


def body(decoder, pair_map, indices, values, target):
    vmem = pl.BlockSpec(memory_space=pltpu.VMEM)
    dma = pltpu.SemaphoreType.DMA
    recon, feat, grad = pl.pallas_call(
        exchange_kernel,
        out_shape=(
            pltpu.VMEM((LAYERS, 16, 128), F32),
            pltpu.VMEM((LAYERS, ACTIVE), F32),
            pltpu.VMEM((WIDTH, MODEL), F32),
        ),
        in_specs=[pl.BlockSpec(memory_space=pltpu.SMEM), vmem, vmem, vmem, pl.BlockSpec(memory_space=pl.ANY)],
        out_specs=(vmem, vmem, vmem),
        scratch_shapes=[
            pltpu.VMEM((WIDTH, TOK), BF16),
            pltpu.VMEM((WIDTH, TOK), BF16),
            pltpu.VMEM((WIDTH, MODEL), F32),
            pltpu.VMEM((WIDTH, MODEL), BF16),
            pltpu.VMEM((WIDTH, MODEL), BF16),
            pltpu.VMEM((2, ACTIVE, TOK // 2), jnp.int32),
            pltpu.VMEM((2, ACTIVE, TOK // 2), F32),
            pltpu.VMEM((TOK, WIDTH), BF16),
            pltpu.VMEM((8, 128), jnp.int32),
            pltpu.VMEM((PAIRS, 8, 128), jnp.int32),
            pltpu.VMEM((TOK, HALF), F32),
            pltpu.VMEM((TOK, HALF), F32),
            pltpu.VMEM((TOK, HALF), F32),
            pltpu.VMEM((PLANE, 1, 128), F32),
            pltpu.VMEM((PLANE, 1, 128), F32),
            pltpu.VMEM((PLANE, ROWS, HALF), jnp.int16),
            pltpu.VMEM((PLANE, ROWS, HALF), jnp.int16),
            pltpu.VMEM((LAYERS, ROWS, HALF), F32),
            pltpu.VMEM((LINE * 32, 128), F32),
            pltpu.VMEM((LINE, 32, 128), jnp.int16),
            pltpu.VMEM((LINE, 32, 128), jnp.int16),
            pltpu.VMEM((2, 24, 128), BF16),
            pltpu.VMEM((LINE, 24, 128), BF16),
            pltpu.VMEM((LINE * 24, 128), F32),
            pltpu.VMEM((LAYERS, ROWS, HALF), F32),
            pltpu.VMEM((PAIRS, ROWS, HALF), BF16),
            pltpu.VMEM((2, TOK, HALF), BF16),
            pltpu.VMEM((TOK, WIDTH), F32),
            pltpu.VMEM((TOK, ACTIVE), F32),
            pltpu.VMEM((PLANE, ROWS, ACTIVE), F32),
            pltpu.VMEM((LINE * 8, 128), F32),
            pltpu.VMEM((LINE, 4, 128), F32),
            pltpu.VMEM((LINE, 4, 128), F32),
            dma((4,)),
            dma((PAIRS,)), dma((PAIRS,)),
            dma((2,)), dma((2,)),
            dma((PLANE,)), dma((PLANE,)),
            dma((PLANE,)), dma((PLANE,)),
            dma((LINE,)), dma((LINE,)),
            dma((LINE,)), dma((LINE,)),
            dma((PLANE,)), dma((PLANE,)),
            dma((PLANE,)), dma((PLANE,)),
            dma((PLANE,)), dma((PLANE,)),
            dma((LINE,)), dma((LINE,)),
        ],
        compiler_params=pltpu.CompilerParams(
            collective_id=0, has_side_effects=True, vmem_limit_bytes=59 * 2**20
        ),
    )(pair_map, indices, values, target.reshape(LAYERS, 16, 128), decoder)
    dec_grad, recon, feat = pl.pallas_call(
        output_kernel,
        out_shape=(
            jax.ShapeDtypeStruct((WIDTH, MODEL), F32),
            jax.ShapeDtypeStruct((LAYERS, MODEL), BF16),
            jax.ShapeDtypeStruct((LAYERS, 1, ACTIVE), F32),
        ),
        in_specs=[vmem, vmem, vmem],
        out_specs=(pl.BlockSpec(memory_space=pl.ANY), vmem, vmem),
        scratch_shapes=[dma((WIDTH // 128,))],
        compiler_params=pltpu.CompilerParams(vmem_limit_bytes=59 * 2**20),
    )(*(pltpu.with_memory_space_constraint(x, pltpu.VMEM) for x in (grad, recon, feat)))
    return recon.reshape(LAYERS, 1, MODEL), dec_grad.reshape(1, WIDTH, MODEL), feat


def solution(mesh):
    in_specs = (P("pair", "feat", None), P("pair", None), P(), P(), P(None, ("pair", "feat"), None))
    out_specs = (
        P(None, ("pair", "feat"), None),
        P("pair", "feat", None),
        P(None, ("pair", "feat"), None),
    )
    return jax.shard_map(body, mesh=mesh, in_specs=in_specs, out_specs=out_specs, check_vma=False)
```
